128 devices in a mesh: lon: 32 (over x, y, core), lat: 4 (over z).
Axes of the slice: x: 4, y: 4, z: 4, core: 2. Of those that a mesh axis runs over, the one named last changes fastest.
Arguments:
- vel_base: bfloat16 [32, 4, 8, 16, 2, 128], P('lon', 'lat'), may hold values from -1.25 to 1.25
- vel_grad: bfloat16 [32, 4, 8, 16, 4, 128], P('lon', 'lat'), may hold values from -0.29882812 to 0.29882812
- route_dev: int32 [32, 4, 8, 128, 1], P('lon', 'lat'), may hold values from 0 to 127; in each aligned block of 128 rows (0 to 127, 128 to 255, ..., all dimensions but the last counted through in order) at most 2 rows name the same one
- route_block: int32 [32, 4, 8, 128], P('lon', 'lat'), may hold values from 0 to 15
- seed_cells: int32 [8, 2048, 4096], P(None, 'lat', 'lon'), may hold values from 0 to 127
Outputs:
- flow_map: float32 [2, 2048, 4096], P(None, 'lat', 'lon')
- ftle_field: float32 [2048, 4096], P('lat', 'lon')
The draws below stay inside these ranges and needn't reach their ends.
Inputs may be any that keep to these rules, and one draw needn't show every extreme that they name: `route_dev`: in each step, at most 2 of the 128 seed groups of one device name the same owner; in some steps of some devices an owner is named by exactly 2 groups.
All inputs are finite; a program needn't handle non-finite values.
Results may differ from the reference program's by a relative error of at most 0.0003.
Values may be sent and summed in bfloat16 or wider, within the bound.
A program may use at most 64 MiB of HBM per device.

```python
import math
import jax
import jax.numpy as jnp
import numpy as np

SEED_LAT = 512
SEED_LON = 128
GROUP_ROWS = 4
CELLS_PER_BLOCK = 128
BLOCKS_DEV = 16
STEPS = 8
GROUPS = 128
SLOTS = 2
GRID_LAT = 2048
GRID_LON = 4096
N_LON = 32
N_LAT = 4
DEVICES = 128


def set_ends(result, stream_key, low, high):
    shape = result.shape
    index_at = [jax.random.randint(jax.random.fold_in(stream_key, axis), (), 0, shape[axis]) for axis in range(len(shape))]
    result = result.at[tuple(index_at)].set(low)
    longest = shape.index(max(shape))
    index_at[longest] = (index_at[longest] + 1) % shape[longest]
    return result.at[tuple(index_at)].set(high)


def block_scale(rng, extent, pieces, smallest, top_value):
    gain, own = 1.0, jax.random.fold_in(rng, 6)
    for dim, shards_of in pieces:
        draws = jnp.exp(jax.random.uniform(jax.random.fold_in(own, dim), (shards_of,), jnp.float32, smallest / len(pieces), top_value / len(pieces)))
        gain = gain * jnp.repeat(draws, extent[dim] // shards_of).reshape([-1 if axis == dim else 1 for axis in range(len(extent))])
    return gain


def routed_block(rng, own, number, rows, number_of, top, most, slope):
    sequence = jax.random.permutation(rng, number_of)
    heavy_load, usual = load_shares(number_of, rows * top, most, slope, True), load_shares(number_of, rows * top, most, slope, False)
    places = jnp.arange(number_of)

    def named(lengths, turn):
        used = int((lengths > 0).sum())
        fixed = max(1, used // 4)
        moved = fixed + (places - fixed + turn * (used - fixed)) % max(1, number_of - fixed)
        return jnp.zeros((number_of,), jnp.int32).at[sequence[jnp.where(places < fixed, places, moved)]].set(jnp.asarray(lengths, jnp.int32))

    lengths = jnp.where(number % 4 == 0, named(heavy_load, number // 4), named(usual, number - number // 4 - 1))
    mixed = jax.random.permutation(jax.random.fold_in(own, 3), number_of)
    source_of, sink = mixed[0:number_of // 2 * 2:2], mixed[1:number_of // 2 * 2:2]
    room = jnp.minimum(lengths[source_of] - 1, most - lengths[sink]) // 2
    room = jnp.where((source_of == sequence[0]) | (sink == sequence[0]) | (lengths[sink] == 0), 0, jnp.maximum(room, 0))
    moved = jax.random.randint(jax.random.fold_in(own, 4), (number_of // 2,), 0, 1 << 20) % (room + 1)
    lengths = lengths.at[source_of].add(-moved).at[sink].add(moved)
    items = jnp.searchsorted(jnp.cumsum(lengths), jnp.arange(rows * top), side="right").astype(jnp.int32)
    grid = items.reshape(top, rows).T
    grid = grid[jax.random.permutation(jax.random.fold_in(own, 1), rows)]
    turn = jax.random.randint(jax.random.fold_in(own, 2), (rows, 1), 0, top)
    return jnp.take_along_axis(grid, (jnp.arange(top)[None, :] + turn) % top, axis=1)


def load_shares(number_of, total, most, lean, full):
    loads = [(1 << 20) // math.isqrt(standing ** lean) + 1 for standing in range(1, number_of + 1)]
    largest = most if full else min(most, max(-(-total // number_of), total * loads[0] // sum(loads)))
    least = 1 if total - largest >= number_of - 1 else 0
    given, rest = [largest] + [least] * (number_of - 1), total - largest - least * (number_of - 1)
    while rest > 0:
        movable = [i for i in range(1, number_of) if given[i] < largest] or [i for i in range(1, number_of) if given[i] < most]
        mass, budget = sum([loads[i] for i in movable]), rest
        for i in movable:
            more = min(most - given[i], max(1, budget * loads[i] // mass), rest)
            given[i] = given[i] + more
            rest = rest - more
    return np.array(given)


def centred(own_key, dims, width, bound, cuts=(), dtype=jnp.bfloat16):
    level = block_scale(own_key, dims, cuts, -0.22, 0.18) if cuts else 1.0
    result = jax.random.normal(own_key, dims, jnp.float32) * width * level
    return jnp.minimum(jnp.maximum(result, -bound), bound).astype(dtype)


def setup_inputs(seed: int = 0) -> dict:
    key_of = jax.random.split(jax.random.key(seed), 6)
    vel_base = centred(key_of[0], (N_LON, N_LAT, STEPS, BLOCKS_DEV, 2, CELLS_PER_BLOCK), 0.09, 1.25, ((0, 32), (1, 4)))
    vel_grad = jnp.clip(jax.random.uniform(key_of[1], (N_LON, N_LAT, STEPS, BLOCKS_DEV, 4, CELLS_PER_BLOCK), jnp.float32, -0.29882812, 0.29882812) * block_scale(key_of[1], (N_LON, N_LAT, STEPS, BLOCKS_DEV, 4, CELLS_PER_BLOCK), ((0, 32), (1, 4)), -0.4, 0.0), -0.29882812, 0.29882812).astype(jnp.bfloat16)
    route_dev_keys = jax.random.split(jax.random.fold_in(key_of[2], 1), N_LON * N_LAT * STEPS * GROUPS // GROUPS)
    route_dev_turns = jax.random.permutation(jax.random.fold_in(key_of[2], 3), N_LON * N_LAT * STEPS * GROUPS // GROUPS)
    route_dev = jax.vmap(lambda own, number: routed_block(jax.random.fold_in(key_of[2], 2), own, number, GROUPS, DEVICES, 1, SLOTS, 2))(route_dev_keys, route_dev_turns).reshape((N_LON, N_LAT, STEPS, GROUPS, 1))
    route_block = set_ends(jax.random.randint(key_of[3], (N_LON, N_LAT, STEPS, GROUPS), 0, BLOCKS_DEV), jax.random.fold_in(key_of[3], 1), 0, BLOCKS_DEV - 1).astype(jnp.int32)
    seed_cells = set_ends(jax.random.randint(key_of[4], (STEPS, GRID_LAT, GRID_LON), 0, CELLS_PER_BLOCK), jax.random.fold_in(key_of[4], 1), 0, CELLS_PER_BLOCK - 1).astype(jnp.int32)
    return {"vel_base": vel_base, "vel_grad": vel_grad, "route_dev": route_dev, "route_block": route_block, "seed_cells": seed_cells}


def velocity_rate(eastward_component, along_y, coeffs):
    vel_x, vel_y, grad_xx, grad_xy, grad_yx, grad_yy = coeffs
    return (-(vel_x + grad_xx * eastward_component + grad_xy * along_y), -(vel_y + grad_yx * eastward_component + grad_yy * along_y))

def runge_kutta(eastward_component, along_y, coeffs, dt_step):
    half_step = 0.5 * dt_step
    rate_one = velocity_rate(eastward_component, along_y, coeffs)
    rate_two = velocity_rate(eastward_component + half_step * rate_one[0], along_y + half_step * rate_one[1], coeffs)
    rate_three = velocity_rate(eastward_component + half_step * rate_two[0], along_y + half_step * rate_two[1], coeffs)
    rate_four = velocity_rate(eastward_component + dt_step * rate_three[0], along_y + dt_step * rate_three[1], coeffs)
    sixth = dt_step / 6.0
    new_x = eastward_component + sixth * (rate_one[0] + 2.0 * rate_two[0] + 2.0 * rate_three[0] + rate_four[0])
    new_y = along_y + sixth * (rate_one[1] + 2.0 * rate_two[1] + 2.0 * rate_three[1] + rate_four[1])
    return (new_x, new_y)

def stretch_rate(diff_lon, diff_lat):
    map_xx = 1.0 + diff_lon[0]
    map_xy = diff_lat[0]
    map_yx = diff_lon[1]
    map_yy = 1.0 + diff_lat[1]
    green_xx = map_xx * map_xx + map_yx * map_yx
    green_yy = map_xy * map_xy + map_yy * map_yy
    green_xy = map_xx * map_xy + map_yx * map_yy
    half_diff = 0.5 * (green_xx - green_yy)
    largest = 0.5 * (green_xx + green_yy) + jnp.sqrt(half_diff * half_diff + green_xy * green_xy)
    return 0.5 * jnp.log(largest)

def arrange(route_table):
    lat_groups = SEED_LAT // GROUP_ROWS
    lon_groups = SEED_LON // 128
    shaped = route_table.reshape(N_LON, N_LAT, STEPS, lat_groups, lon_groups)
    shaped = jnp.transpose(shaped, (2, 1, 3, 0, 4))
    return shaped.reshape(STEPS, N_LAT * lat_groups, N_LON * lon_groups)

def reference(vel_base, vel_grad, route_dev, route_block, seed_cells):
    owners = arrange(route_dev[..., 0]).astype(jnp.int32)
    blocks = arrange(route_block).astype(jnp.int32)
    vel_table = jnp.concatenate([vel_base, vel_grad], axis=4).reshape(-1)
    dt_step = 1.0 / STEPS
    eastward_component = jnp.zeros((GRID_LAT, GRID_LON), jnp.float32)
    along_y = jnp.zeros((GRID_LAT, GRID_LON), jnp.float32)
    for step_index in range(STEPS):
        block_id = (owners[step_index] * STEPS + step_index) * BLOCKS_DEV + blocks[step_index]
        block_id = jnp.repeat(jnp.repeat(block_id, GROUP_ROWS, axis=0), 128, axis=1)
        offset = (block_id * (6 * CELLS_PER_BLOCK) + seed_cells[step_index]).astype(jnp.int32)
        coeffs = tuple((jnp.take(vel_table, offset + component * CELLS_PER_BLOCK).astype(jnp.float32) for component in range(6)))
        eastward_component, along_y = runge_kutta(eastward_component, along_y, coeffs, dt_step)
    flow_map = jnp.stack([eastward_component, along_y])
    diff_lon = (jnp.roll(flow_map, -1, axis=2) - jnp.roll(flow_map, 1, axis=2)) * 0.5
    padded = jnp.pad(flow_map, ((0, 0), (1, 1), (0, 0)), mode='edge')
    diff_lat = (padded[:, 2:] - padded[:, :-2]) * 0.5
    return (flow_map, stretch_rate(diff_lon, diff_lat))
```

```python
import jax
import jax.numpy as jnp
from jax import lax
from jax.experimental import pallas as pl
from jax.experimental.pallas import tpu as pltpu
from jax.sharding import PartitionSpec as P

MESH = pl.DeviceIdType.MESH
STEPS = 8
CHUNKS = 2
PER = STEPS // CHUNKS
GROUPS = 128
GROUP_ROWS = 4
BLOCKS = 16
WIDTH = 256
DIMS = ((1, 2, 0), (2, 0, 1), (0, 1, 2))


def owner_parts(owner):
    return (owner >> 5) & 3, (owner >> 3) & 3, owner & 3, (owner >> 2) & 1


def owner_number(place, core):
    return place[0] * 32 + place[1] * 8 + core * 4 + place[2]


def kernel(
    table_ref, dev_ref, block_ref, cells_hbm, flow_ref, ftle_ref,
    tab, rep, rcv, cells, pick, sort, ask, asked, first, state, coef,
    rows_out, rows_in, cols_out, cols_in,
    cell_sem, own_sem, back_sem, send1, recv1, send2, recv2, send3, recv3, sendq, recvq, sendh, recvh,
):
    lon = lax.axis_index("lon")
    lat = lax.axis_index("lat")
    core = lon % 2
    here = (lon // 8, (lon // 2) % 4, lat)
    n_lon = 32

    def device(place, which):
        return ((place[0] * 4 + place[1]) * 2 + which, place[2])

    def moved(dim, by):
        place = list(here)
        place[dim] = (place[dim] + by) % 4
        return place

    east, west = (lon + 1) % n_lon, (lon + n_lon - 1) % n_lon
    partners = [device(moved(dim, by), (core + flip) % 2) for dim in range(3) for by in (1, 2, 3) for flip in (0, 1)]
    partners += [device(here, 1 - core), (east, lat), (west, lat)]

    cells_copy = pltpu.make_async_copy(cells_hbm, cells, cell_sem)
    cells_copy.start()
    own = []
    for k, (d1, d2, _) in enumerate(DIMS):
        for c in range(CHUNKS):
            own.append(
                pltpu.make_async_copy(
                    table_ref.at[k, pl.ds(c * PER, PER)], tab.at[k, c, here[d2], here[d1]], own_sem.at[k, c]
                )
            )
            own[-1].start()

    barrier = pltpu.get_barrier_semaphore()
    for partner in partners:
        pl.semaphore_signal(barrier, inc=1, device_id=partner, device_id_type=MESH)
    pl.semaphore_wait(barrier, len(partners))

    def remote(src, dst, send, recv, target):
        return pltpu.make_async_remote_copy(
            src_ref=src, dst_ref=dst, send_sem=send, recv_sem=recv, device_id=target, device_id_type=MESH
        )

    phase1, phase2, phase3, query, back = {}, {}, {}, {}, {}
    for c in range(CHUNKS):
        for k, (d1, d2, d3) in enumerate(DIMS):
            for by in (1, 3, 2):
                phase1[k, c, by] = remote(
                    table_ref.at[k, pl.ds(c * PER, PER)], tab.at[k, c, here[d2], here[d1]],
                    send1.at[k, c, by - 1], recv1.at[k, c, by - 1], device(moved(d1, by), core),
                )
                phase2[k, c, by] = remote(
                    tab.at[k, c, here[d2]], tab.at[k, c, here[d2]],
                    send2.at[k, c, by - 1], recv2.at[k, c, by - 1], device(moved(d2, by), core),
                )
            mine = here[d3] * 2 + core
            for i, (by, flip) in enumerate(((1, 0), (3, 0), (2, 0), (1, 1), (3, 1), (2, 1), (0, 1))):
                place, which = moved(d3, by), (core + flip) % 2
                theirs = place[d3] * 2 + which
                phase3[k, c, i] = remote(
                    rep.at[k, c, theirs], rcv.at[k, c, mine], send3.at[k, c, i], recv3.at[k, c, i], device(place, which)
                )
                if c == 0:
                    query[k, i] = remote(
                        ask.at[k, theirs // 4], asked.at[k, mine], sendq.at[k, i], recvq.at[k, i], device(place, which)
                    )
            back[k, c] = pltpu.make_async_copy(rep.at[k, c, mine], rcv.at[k, c, mine], back_sem.at[k, c])

    for c in range(CHUNKS):
        for by in (1, 3, 2):
            for k in range(3):
                phase1[k, c, by].start()

    lane = lax.broadcasted_iota(jnp.int32, (GROUPS, 128), 1)
    group = lax.broadcasted_iota(jnp.int32, (GROUPS, 128), 0)
    dev_columns = jnp.transpose(dev_ref[...].astype(jnp.float32))
    block_columns = jnp.transpose(block_ref[...].astype(jnp.float32))
    lane_f, group_f = lane.astype(jnp.float32), group.astype(jnp.float32)
    for s in range(STEPS):
        named = jnp.broadcast_to(dev_columns[:, s : s + 1], (GROUPS, 128)) == lane_f
        value = group_f * BLOCKS + jnp.broadcast_to(block_columns[:, s : s + 1], (GROUPS, 128))
        last = jnp.max(jnp.where(named, value, -1.0), axis=0, keepdims=True)
        least = jnp.min(jnp.where(named, value, 1e6), axis=0, keepdims=True)
        first[0, s : s + 1, :] = jnp.where(last >= 0.0, last - BLOCKS * jnp.floor(last * (1.0 / BLOCKS)), -1e4)
        first[1, s : s + 1, :] = jnp.where(least < last, least - BLOCKS * jnp.floor(least * (1.0 / BLOCKS)), -1e4)
    wide = lax.broadcasted_iota(jnp.int32, (8, 128), 1)
    for k, (d1, d2, d3) in enumerate(DIMS):
        for half in range(2):
            place = [None] * 3
            number = wide + half * 128
            place[d1], place[d2], place[d3] = (number >> 1) & 3, (number >> 3) & 3, (number >> 6) & 3
            index = owner_number(place, (number >> 5) & 1)
            chosen = jnp.where(
                (number & 1) == 0,
                jnp.take_along_axis(first[0], index, axis=1, mode="promise_in_bounds"),
                jnp.take_along_axis(first[1], index, axis=1, mode="promise_in_bounds"),
            )
            ask[k, half] = chosen + (((number >> 1) & 15) * BLOCKS).astype(jnp.float32)
        for i in range(7):
            query[k, i].start()
        asked[k, here[d3] * 2 + core] = ask[k, here[d3] // 2]

    for c in range(CHUNKS):
        for k in range(3):
            own[k * CHUNKS + c].wait()
            for by in (1, 3, 2):
                phase1[k, c, by].wait_recv()
            for by in (1, 3, 2):
                phase2[k, c, by].start()

    dev_int = dev_columns.astype(jnp.int32)
    slot_lane = lax.broadcasted_iota(jnp.int32, (GROUPS, WIDTH), 1)
    for s in range(STEPS):
        same = (jnp.broadcast_to(dev_columns[:, s : s + 1], (GROUPS, 128)) == dev_ref[s : s + 1, :].astype(jnp.float32)) & (
            lane > group
        )
        rank = jnp.max(jnp.where(same, 1.0, 0.0), axis=1, keepdims=True).astype(jnp.int32)
        x, y, z, which = owner_parts(dev_int[:, s : s + 1])
        place = (x, y, z)
        for k, (d1, d2, d3) in enumerate(DIMS):
            slot = (((place[d3] * 2 + which) * 4 + place[d2]) * 4 + place[d1]) * 2 + rank
            sort[k, s] = jnp.where(jnp.broadcast_to(slot, (GROUPS, WIDTH)) == slot_lane, -1.0 / STEPS, 0.0).astype(jnp.bfloat16)

    block_lane = lax.broadcasted_iota(jnp.int32, (WIDTH, WIDTH), 1).astype(jnp.float32)
    for k, (_, _, d3) in enumerate(DIMS):
        for i in range(7):
            query[k, i].wait_recv()
        window = (here[d3] * 2 + core) % 4
        halves = []
        for half in range(2):
            total = jnp.full((8, 128), -1e4, jnp.float32)
            for r in range(4):
                turned = pltpu.roll(asked[k, half * 4 + r], (r - window + 4) % 4 * 32, 1)
                total = jnp.where(wide // 32 == r, turned, total)
            halves.append(jnp.transpose(total))
        rows = jnp.concatenate(halves, axis=0)
        for s in range(STEPS):
            pick[k, s] = jnp.where(
                jnp.broadcast_to(rows[:, s : s + 1], (WIDTH, WIDTH)) == block_lane, 1.0, 0.0
            ).astype(jnp.bfloat16)

    for c in range(CHUNKS):
        for k in range(3):
            for by in (1, 3, 2):
                phase2[k, c, by].wait_recv()

            @pl.loop(0, PER)
            def _(j):
                found = jnp.dot(
                    pick[k, c * PER + j], tab[k, c, :, :, j].reshape(WIDTH, WIDTH), preferred_element_type=jnp.float32
                )
                rep[k, c, :, j] = found.astype(jnp.bfloat16).reshape(8, 32, WIDTH)

            for i in range(7):
                phase3[k, c, i].start()
            back[k, c].start()

    state[...] = jnp.zeros_like(state)
    cells_copy.wait()
    for c in range(CHUNKS):
        for k in range(3):
            back[k, c].wait()
            for i in range(7):
                phase3[k, c, i].wait_recv()

        @pl.loop(0, PER)
        def _(j):
            step = c * PER + j
            for k in range(3):
                found = jnp.dot(
                    sort[k, step], rcv[k, c, :, j].reshape(WIDTH, WIDTH), preferred_element_type=jnp.float32
                )
                coef[2 * k] = found[:, :128]
                coef[2 * k + 1] = found[:, 128:]

            @pl.loop(0, GROUPS // 8)
            def _(t):
                start = pl.multiple_of(t * 8, 8)
                tables = [coef[m, pl.ds(start, 8), :] for m in range(6)]
                for q in range(GROUP_ROWS):
                    index = cells[step, pl.ds(t * 32 + q, 8, stride=GROUP_ROWS), :]
                    vx, vy, gxx, gxy, gyx, gyy = (
                        jnp.take_along_axis(table, index, axis=1, mode="promise_in_bounds") for table in tables
                    )
                    px, py = state[0, q, pl.ds(start, 8), :], state[1, q, pl.ds(start, 8), :]
                    kx = vx + (gxx * px + gxy * py)
                    ky = vy + (gyx * px + gyy * py)
                    wx, wy = kx, ky
                    for part in (0.25, 1.0 / 3.0, 0.5):
                        wx, wy = kx + part * (gxx * wx + gxy * wy), ky + part * (gyx * wx + gyy * wy)
                    state[0, q, pl.ds(start, 8), :] = px + wx
                    state[1, q, pl.ds(start, 8), :] = py + wy

    rows_out[...] = jnp.zeros_like(rows_out)
    cols_out[...] = jnp.zeros_like(cols_out)
    for comp in range(2):
        rows_out[comp : comp + 1, :] = state[comp, 0, 0:1, :]
        rows_out[2 + comp : 3 + comp, :] = state[comp, GROUP_ROWS - 1, GROUPS - 1 : GROUPS, :]
    halo = []
    for i, by in enumerate((1, 3)):
        halo.append(remote(rows_out, rows_in.at[i], sendh.at[i], recvh.at[i], device(moved(2, by), core)))
        halo[-1].start()
    for comp in range(2):
        for q in range(GROUP_ROWS):
            turned = jnp.transpose(state[comp, q])
            cols_out[q, comp : comp + 1, :] = turned[0:1, :]
            cols_out[q, 2 + comp : 3 + comp, :] = turned[127:128, :]
    for i, lon_to in enumerate((east, west)):
        halo.append(remote(cols_out, cols_in.at[i], sendh.at[2 + i], recvh.at[2 + i], (lon_to, lat)))
        halo[-1].start()
    for comp in range(2):
        for q in range(GROUP_ROWS):
            flow_ref[comp, pl.ds(q, GROUPS, stride=GROUP_ROWS), :] = state[comp, q]
    for copy in halo:
        copy.wait_recv()
    south_own, north_own = lat == 0, lat == 3
    at_west, at_east = lane == 0, lane == 127
    bottom, top = group == 0, group == GROUPS - 1
    diffs = {}
    for comp in range(2):
        south = jnp.where(south_own, rows_out[comp : comp + 1, :], rows_in[0, 2 + comp : 3 + comp, :])
        north = jnp.where(north_own, rows_out[2 + comp : 3 + comp, :], rows_in[1, comp : comp + 1, :])
        for q in range(GROUP_ROWS):
            own_rows = state[comp, q]
            west_column = jnp.transpose(cols_in[0, q])[:, 2 + comp : 3 + comp]
            east_column = jnp.transpose(cols_in[1, q])[:, comp : comp + 1]
            low = jnp.where(at_west, west_column, pltpu.roll(own_rows, 1, 1))
            high = jnp.where(at_east, east_column, pltpu.roll(own_rows, 127, 1))
            diffs[comp, q, 0] = (high - low) * 0.5
            if q == 0:
                below = jnp.where(bottom, south, pltpu.roll(state[comp, GROUP_ROWS - 1], 1, 0))
            else:
                below = state[comp, q - 1]
            if q == GROUP_ROWS - 1:
                above = jnp.where(top, north, pltpu.roll(state[comp, 0], GROUPS - 1, 0))
            else:
                above = state[comp, q + 1]
            diffs[comp, q, 1] = (above - below) * 0.5
    for q in range(GROUP_ROWS):
        map_xx, map_yx = 1.0 + diffs[0, q, 0], diffs[1, q, 0]
        map_xy, map_yy = diffs[0, q, 1], 1.0 + diffs[1, q, 1]
        green_xx = map_xx * map_xx + map_yx * map_yx
        green_yy = map_xy * map_xy + map_yy * map_yy
        green_xy = map_xx * map_xy + map_yx * map_yy
        half_diff = 0.5 * (green_xx - green_yy)
        largest = 0.5 * (green_xx + green_yy) + jnp.sqrt(half_diff * half_diff + green_xy * green_xy)
        ftle_ref[pl.ds(q, GROUPS, stride=GROUP_ROWS), :] = 0.5 * jnp.log(largest)

    for copies in (phase1, phase2, phase3, query):
        for copy in copies.values():
            copy.wait_send()
    for copy in halo:
        copy.wait_send()


def body(vel_base, vel_grad, route_dev, route_block, seed_cells):
    table = jnp.concatenate([vel_base[0, 0], vel_grad[0, 0]], axis=2).reshape(STEPS, BLOCKS, 3, WIDTH)
    table = jnp.transpose(table, (2, 0, 1, 3))
    dma = pltpu.SemaphoreType.DMA
    vmem = pl.BlockSpec(memory_space=pltpu.VMEM)
    return pl.pallas_call(
        kernel,
        out_shape=(
            jax.ShapeDtypeStruct((2, 512, 128), jnp.float32),
            jax.ShapeDtypeStruct((512, 128), jnp.float32),
        ),
        in_specs=[vmem, vmem, vmem, pl.BlockSpec(memory_space=pl.ANY)],
        out_specs=(vmem, vmem),
        scratch_shapes=[
            pltpu.VMEM((3, CHUNKS, 4, 4, PER, BLOCKS, WIDTH), jnp.bfloat16),
            pltpu.VMEM((3, CHUNKS, 8, PER, 32, WIDTH), jnp.bfloat16),
            pltpu.VMEM((3, CHUNKS, 8, PER, 32, WIDTH), jnp.bfloat16),
            pltpu.VMEM((STEPS, 512, 128), jnp.int32),
            pltpu.VMEM((3, STEPS, WIDTH, WIDTH), jnp.bfloat16),
            pltpu.VMEM((3, STEPS, GROUPS, WIDTH), jnp.bfloat16),
            pltpu.VMEM((3, 2, 8, 128), jnp.float32),
            pltpu.VMEM((3, 8, 8, 128), jnp.float32),
            pltpu.VMEM((2, STEPS, 128), jnp.float32),
            pltpu.VMEM((2, GROUP_ROWS, GROUPS, 128), jnp.float32),
            pltpu.VMEM((6, GROUPS, 128), jnp.float32),
            pltpu.VMEM((8, 128), jnp.float32),
            pltpu.VMEM((2, 8, 128), jnp.float32),
            pltpu.VMEM((GROUP_ROWS, 8, 128), jnp.float32),
            pltpu.VMEM((2, GROUP_ROWS, 8, 128), jnp.float32),
            dma, dma((3, CHUNKS)), dma((3, CHUNKS)),
            dma((3, CHUNKS, 3)), dma((3, CHUNKS, 3)),
            dma((3, CHUNKS, 3)), dma((3, CHUNKS, 3)),
            dma((3, CHUNKS, 7)), dma((3, CHUNKS, 7)),
            dma((3, 7)), dma((3, 7)),
            dma((4,)), dma((4,)),
        ],
        compiler_params=pltpu.CompilerParams(
            collective_id=0, has_side_effects=True, vmem_limit_bytes=48 << 20
        ),
    )(table, route_dev[0, 0, :, :, 0], route_block[0, 0], seed_cells)


def solution(mesh):
    in_specs = (
        P("lon", "lat", None, None, None, None),
        P("lon", "lat", None, None, None, None),
        P("lon", "lat", None, None, None),
        P("lon", "lat", None, None),
        P(None, "lat", "lon"),
    )
    out_specs = (P(None, "lat", "lon"), P("lat", "lon"))
    return jax.shard_map(body, mesh=mesh, in_specs=in_specs, out_specs=out_specs, check_vma=False)
```

```python
import jax
import jax.numpy as jnp
from jax import lax
from jax.experimental import pallas as pl
from jax.experimental.pallas import tpu as pltpu
from jax.sharding import PartitionSpec as P

MESH = pl.DeviceIdType.MESH
STEPS = 8
GROUPS = 128
GROUP_ROWS = 4
BLOCKS = 16
WIDTH = 256
DIMS = ((1, 2, 0), (2, 0, 1), (0, 1, 2))
PIECES1 = ((0, 2), (2, 6))
PIECES = ((0, 2), (2, 2), (4, 2), (6, 2))
NEAR = (1, 3, 2)
LINE = ((1, 0), (3, 0), (2, 0), (1, 1), (3, 1), (2, 1), (0, 1))


def owner_parts(owner):
    return (owner >> 5) & 3, (owner >> 3) & 3, owner & 3, (owner >> 2) & 1


def owner_number(place, core):
    return place[0] * 32 + place[1] * 8 + core * 4 + place[2]


def advect_kernel(
    base_hbm, grad_hbm, dev_hbm, block_hbm, cells_hbm, state, rows_in, cols_in, rows_out,
    base, grad, dev_ref, block_ref, cells, tab, rep, rcv, pick, sort, ask, asked, first, coef, cols_out,
    load_sem, back_sem, send1, recv1, send2, recv2, send3, recv3, sendq, recvq, sendh, recvh,
):
    lon = lax.axis_index("lon")
    lat = lax.axis_index("lat")
    core = lon % 2
    here = (lon // 8, (lon // 2) % 4, lat)
    n_lon = 32

    def device(place, which):
        return ((place[0] * 4 + place[1]) * 2 + which, place[2])

    def moved(dim, by):
        place = list(here)
        place[dim] = (place[dim] + by) % 4
        return place

    east, west = (lon + 1) % n_lon, (lon + n_lon - 1) % n_lon
    partners = [device(moved(dim, by), (core + flip) % 2) for dim in range(3) for by in (1, 2, 3) for flip in (0, 1)]
    partners += [device(here, 1 - core), (east, lat), (west, lat)]
    barrier = pltpu.get_barrier_semaphore()
    for partner in partners:
        pl.semaphore_signal(barrier, inc=1, device_id=partner, device_id_type=MESH)

    loads = [
        pltpu.make_async_copy(src, dst, load_sem.at[i])
        for i, (src, dst) in enumerate(
            ((base_hbm, base), (grad_hbm, grad), (dev_hbm, dev_ref), (block_hbm, block_ref), (cells_hbm, cells))
        )
    ]
    for load in loads:
        load.start()

    row = lax.broadcasted_iota(jnp.int32, (256, 256), 0)
    column = lax.broadcasted_iota(jnp.int32, (256, 256), 1)
    order = jnp.where(column == (row & 127) * 2 + (row >> 7), 1.0, 0.0).astype(jnp.bfloat16)
    loads[0].wait()
    mine = jnp.dot(order, base[...], preferred_element_type=jnp.float32).astype(jnp.bfloat16)
    for m in range(2):
        part = mine[m * 128 : (m + 1) * 128].reshape(STEPS, BLOCKS, 128)
        tab[0, :, here[DIMS[0][1]], here[DIMS[0][0]], :, m * 128 : (m + 1) * 128] = part
    order = jnp.where(column == (row & 63) * 4 + (row >> 6), 1.0, 0.0).astype(jnp.bfloat16)
    loads[1].wait()
    for half in range(2):
        mine = jnp.dot(
            order, grad[half * 256 : (half + 1) * 256], preferred_element_type=jnp.float32
        ).astype(jnp.bfloat16)
        for m in range(4):
            k = 1 + m // 2
            part = mine[m * 64 : (m + 1) * 64].reshape(4, BLOCKS, 128)
            tab[
                k, half * 4 : half * 4 + 4, here[DIMS[k][1]], here[DIMS[k][0]], :, m % 2 * 128 : m % 2 * 128 + 128
            ] = part
    pl.semaphore_wait(barrier, len(partners))

    def remote(src, dst, send, recv, target):
        return pltpu.make_async_remote_copy(
            src_ref=src, dst_ref=dst, send_sem=send, recv_sem=recv, device_id=target, device_id_type=MESH
        )

    phase1, phase2, phase3, query, back = {}, {}, {}, {}, {}
    for k, (d1, d2, d3) in enumerate(DIMS):
        for c, (s0, n) in enumerate(PIECES1):
            for by in NEAR:
                ref = tab.at[k, pl.ds(s0, n), here[d2], here[d1]]
                phase1[k, c, by] = remote(
                    ref, ref, send1.at[k, c, by - 1], recv1.at[k, c, by - 1], device(moved(d1, by), core)
                )
        slot = here[d3] * 2 + core
        for c, (s0, n) in enumerate(PIECES):
            for by in NEAR:
                ref = tab.at[k, pl.ds(s0, n), here[d2]]
                phase2[k, c, by] = remote(
                    ref, ref, send2.at[k, c, by - 1], recv2.at[k, c, by - 1], device(moved(d2, by), core)
                )
            for i, (by, flip) in enumerate(LINE):
                place, which = moved(d3, by), (core + flip) % 2
                theirs = place[d3] * 2 + which
                phase3[k, c, i] = remote(
                    rep.at[k, pl.ds(s0, n), theirs], rcv.at[k, pl.ds(s0, n), slot],
                    send3.at[k, c, i], recv3.at[k, c, i], device(place, which),
                )
                if c == 0:
                    query[k, i] = remote(
                        ask.at[k, theirs // 4], asked.at[k, slot], sendq.at[k, i], recvq.at[k, i], device(place, which)
                    )
            back[k, c] = pltpu.make_async_copy(
                rep.at[k, pl.ds(s0, n), slot], rcv.at[k, pl.ds(s0, n), slot], back_sem.at[k, c]
            )

    for c in range(len(PIECES1)):
        for by in NEAR:
            for k in range(3):
                phase1[k, c, by].start()

    loads[2].wait()
    loads[3].wait()
    lane = lax.broadcasted_iota(jnp.int32, (GROUPS, 128), 1)
    group = lax.broadcasted_iota(jnp.int32, (GROUPS, 128), 0)
    dev_columns = jnp.transpose(dev_ref[...].astype(jnp.float32))
    block_columns = jnp.transpose(block_ref[...].astype(jnp.float32))
    lane_f, group_f = lane.astype(jnp.float32), group.astype(jnp.float32)
    for s in range(STEPS):
        named = jnp.broadcast_to(dev_columns[:, s : s + 1], (GROUPS, 128)) == lane_f
        value = group_f * BLOCKS + jnp.broadcast_to(block_columns[:, s : s + 1], (GROUPS, 128))
        last = jnp.max(jnp.where(named, value, -1.0), axis=0, keepdims=True)
        least = jnp.min(jnp.where(named, value, 1e6), axis=0, keepdims=True)
        first[0, s : s + 1, :] = jnp.where(last >= 0.0, last - BLOCKS * jnp.floor(last * (1.0 / BLOCKS)), -1e4)
        first[1, s : s + 1, :] = jnp.where(least < last, least - BLOCKS * jnp.floor(least * (1.0 / BLOCKS)), -1e4)
    wide = lax.broadcasted_iota(jnp.int32, (8, 128), 1)
    for k, (d1, d2, d3) in enumerate(DIMS):
        for half in range(2):
            place = [None] * 3
            number = wide + half * 128
            place[d1], place[d2], place[d3] = (number >> 1) & 3, (number >> 3) & 3, (number >> 6) & 3
            index = owner_number(place, (number >> 5) & 1)
            chosen = jnp.where(
                (number & 1) == 0,
                jnp.take_along_axis(first[0], index, axis=1, mode="promise_in_bounds"),
                jnp.take_along_axis(first[1], index, axis=1, mode="promise_in_bounds"),
            )
            ask[k, half] = chosen + (((number >> 1) & 15) * BLOCKS).astype(jnp.float32)
        for i in range(7):
            query[k, i].start()
        asked[k, here[d3] * 2 + core] = ask[k, here[d3] // 2]

    arrived = 0
    for c, (s0, n) in enumerate(PIECES):
        while arrived < len(PIECES1) and PIECES1[arrived][0] < s0 + n:
            for k in range(3):
                for by in NEAR:
                    phase1[k, arrived, by].wait_recv()
            arrived += 1
        for by in NEAR:
            for k in range(3):
                phase2[k, c, by].start()

    dev_int = dev_columns.astype(jnp.int32)
    slot_lane = lax.broadcasted_iota(jnp.int32, (GROUPS, WIDTH), 1)
    for s in range(STEPS):
        same = (jnp.broadcast_to(dev_columns[:, s : s + 1], (GROUPS, 128)) == dev_ref[s : s + 1, :].astype(jnp.float32)) & (
            lane > group
        )
        rank = jnp.max(jnp.where(same, 1.0, 0.0), axis=1, keepdims=True).astype(jnp.int32)
        x, y, z, which = owner_parts(dev_int[:, s : s + 1])
        place = (x, y, z)
        for k, (d1, d2, d3) in enumerate(DIMS):
            slot = (((place[d3] * 2 + which) * 4 + place[d2]) * 4 + place[d1]) * 2 + rank
            sort[k, s] = jnp.where(jnp.broadcast_to(slot, (GROUPS, WIDTH)) == slot_lane, -1.0 / STEPS, 0.0).astype(jnp.bfloat16)

    block_lane = lax.broadcasted_iota(jnp.int32, (WIDTH, WIDTH), 1).astype(jnp.float32)
    for k, (_, _, d3) in enumerate(DIMS):
        for i in range(7):
            query[k, i].wait_recv()
        window = (here[d3] * 2 + core) % 4
        halves = []
        for half in range(2):
            total = jnp.full((8, 128), -1e4, jnp.float32)
            for r in range(4):
                turned = pltpu.roll(asked[k, half * 4 + r], (r - window + 4) % 4 * 32, 1)
                total = jnp.where(wide // 32 == r, turned, total)
            halves.append(jnp.transpose(total))
        rows = jnp.concatenate(halves, axis=0)
        for s in range(STEPS):
            pick[k, s] = jnp.where(
                jnp.broadcast_to(rows[:, s : s + 1], (WIDTH, WIDTH)) == block_lane, 1.0, 0.0
            ).astype(jnp.bfloat16)

    for c, (s0, n) in enumerate(PIECES):
        for k in range(3):
            for by in NEAR:
                phase2[k, c, by].wait_recv()
            for s in range(s0, s0 + n):
                found = jnp.dot(pick[k, s], tab[k, s].reshape(WIDTH, WIDTH), preferred_element_type=jnp.float32)
                rep[k, s] = found.astype(jnp.bfloat16).reshape(8, 32, WIDTH)
            for i in range(7):
                phase3[k, c, i].start()
            back[k, c].start()

    state[...] = jnp.zeros_like(state)
    loads[4].wait()
    for c, (s0, n) in enumerate(PIECES):
        for k in range(3):
            back[k, c].wait()
            for i in range(7):
                phase3[k, c, i].wait_recv()

        @pl.loop(s0, s0 + n)
        def _(step):
            for k in range(3):
                found = jnp.dot(sort[k, step], rcv[k, step].reshape(WIDTH, WIDTH), preferred_element_type=jnp.float32)
                coef[2 * k] = found[:, :128]
                coef[2 * k + 1] = found[:, 128:]
            for start in range(0, GROUPS, 8):
                tables = [coef[m, start : start + 8, :] for m in range(6)]
                for q in range(GROUP_ROWS):
                    index = cells[step, pl.ds(start * GROUP_ROWS + q, 8, stride=GROUP_ROWS), :]
                    vx, vy, gxx, gxy, gyx, gyy = (
                        jnp.take_along_axis(table, index, axis=1, mode="promise_in_bounds") for table in tables
                    )
                    px, py = state[0, q, start : start + 8, :], state[1, q, start : start + 8, :]
                    kx = vx + (gxx * px + gxy * py)
                    ky = vy + (gyx * px + gyy * py)
                    wx, wy = kx, ky
                    for part in (0.25, 1.0 / 3.0, 0.5):
                        wx, wy = kx + part * (gxx * wx + gxy * wy), ky + part * (gyx * wx + gyy * wy)
                    state[0, q, start : start + 8, :] = px + wx
                    state[1, q, start : start + 8, :] = py + wy

    rows_out[...] = jnp.zeros_like(rows_out)
    cols_out[...] = jnp.zeros_like(cols_out)
    for comp in range(2):
        rows_out[comp : comp + 1, :] = state[comp, 0, 0:1, :]
        rows_out[2 + comp : 3 + comp, :] = state[comp, GROUP_ROWS - 1, GROUPS - 1 : GROUPS, :]
    halo = []
    for i, by in enumerate((1, 3)):
        halo.append(remote(rows_out, rows_in.at[i], sendh.at[i], recvh.at[i], device(moved(2, by), core)))
        halo[-1].start()
    for comp in range(2):
        for q in range(GROUP_ROWS):
            turned = jnp.transpose(state[comp, q])
            cols_out[q, comp : comp + 1, :] = turned[0:1, :]
            cols_out[q, 2 + comp : 3 + comp, :] = turned[127:128, :]
    for i, lon_to in enumerate((east, west)):
        halo.append(remote(cols_out, cols_in.at[i], sendh.at[2 + i], recvh.at[2 + i], (lon_to, lat)))
        halo[-1].start()
    for copies in (phase1, phase2, phase3, query):
        for copy in copies.values():
            copy.wait_send()
    for copy in halo:
        copy.wait_send()
        copy.wait_recv()


def stretch_kernel(state, rows_in, cols_in, rows_out, flow_hbm, ftle_hbm, flow, ftle, sem):
    lat = lax.axis_index("lat")
    for comp in range(2):
        for q in range(GROUP_ROWS):
            flow[comp, pl.ds(q, GROUPS, stride=GROUP_ROWS), :] = state[comp, q]
    flow_copy = pltpu.make_async_copy(flow, flow_hbm, sem.at[0])
    flow_copy.start()
    lane = lax.broadcasted_iota(jnp.int32, (GROUPS, 128), 1)
    group = lax.broadcasted_iota(jnp.int32, (GROUPS, 128), 0)
    south_own, north_own = lat == 0, lat == 3
    at_west, at_east = lane == 0, lane == 127
    bottom, top = group == 0, group == GROUPS - 1
    diffs = {}
    for comp in range(2):
        south = jnp.where(south_own, rows_out[comp : comp + 1, :], rows_in[0, 2 + comp : 3 + comp, :])
        north = jnp.where(north_own, rows_out[2 + comp : 3 + comp, :], rows_in[1, comp : comp + 1, :])
        for q in range(GROUP_ROWS):
            own_rows = state[comp, q]
            west_column = jnp.transpose(cols_in[0, q])[:, 2 + comp : 3 + comp]
            east_column = jnp.transpose(cols_in[1, q])[:, comp : comp + 1]
            low = jnp.where(at_west, west_column, pltpu.roll(own_rows, 1, 1))
            high = jnp.where(at_east, east_column, pltpu.roll(own_rows, 127, 1))
            diffs[comp, q, 0] = (high - low) * 0.5
            if q == 0:
                below = jnp.where(bottom, south, pltpu.roll(state[comp, GROUP_ROWS - 1], 1, 0))
            else:
                below = state[comp, q - 1]
            if q == GROUP_ROWS - 1:
                above = jnp.where(top, north, pltpu.roll(state[comp, 0], GROUPS - 1, 0))
            else:
                above = state[comp, q + 1]
            diffs[comp, q, 1] = (above - below) * 0.5
    for q in range(GROUP_ROWS):
        map_xx, map_yx = 1.0 + diffs[0, q, 0], diffs[1, q, 0]
        map_xy, map_yy = diffs[0, q, 1], 1.0 + diffs[1, q, 1]
        green_xx = map_xx * map_xx + map_yx * map_yx
        green_yy = map_xy * map_xy + map_yy * map_yy
        green_xy = map_xx * map_xy + map_yx * map_yy
        half_diff = 0.5 * (green_xx - green_yy)
        largest = 0.5 * (green_xx + green_yy) + jnp.sqrt(half_diff * half_diff + green_xy * green_xy)
        ftle[pl.ds(q, GROUPS, stride=GROUP_ROWS), :] = 0.5 * jnp.log(largest)
    ftle_copy = pltpu.make_async_copy(ftle, ftle_hbm, sem.at[1])
    ftle_copy.start()
    flow_copy.wait()
    ftle_copy.wait()


def body(vel_base, vel_grad, route_dev, route_block, seed_cells):
    dma = pltpu.SemaphoreType.DMA
    vmem = pl.BlockSpec(memory_space=pltpu.VMEM)
    hbm = pl.BlockSpec(memory_space=pltpu.HBM)
    bf16, f32, i32 = jnp.bfloat16, jnp.float32, jnp.int32
    moved = pl.pallas_call(
        advect_kernel,
        out_shape=(
            jax.ShapeDtypeStruct((2, GROUP_ROWS, GROUPS, 128), f32),
            jax.ShapeDtypeStruct((2, 8, 128), f32),
            jax.ShapeDtypeStruct((2, GROUP_ROWS, 8, 128), f32),
            jax.ShapeDtypeStruct((8, 128), f32),
        ),
        in_specs=[hbm] * 5,
        out_specs=(vmem,) * 4,
        scratch_shapes=[
            pltpu.VMEM((256, 128), bf16),
            pltpu.VMEM((512, 128), bf16),
            pltpu.VMEM((STEPS, GROUPS), i32),
            pltpu.VMEM((STEPS, GROUPS), i32),
            pltpu.VMEM((STEPS, 512, 128), i32),
            pltpu.VMEM((3, STEPS, 4, 4, BLOCKS, WIDTH), bf16),
            pltpu.VMEM((3, STEPS, 8, 32, WIDTH), bf16),
            pltpu.VMEM((3, STEPS, 8, 32, WIDTH), bf16),
            pltpu.VMEM((3, STEPS, WIDTH, WIDTH), bf16),
            pltpu.VMEM((3, STEPS, GROUPS, WIDTH), bf16),
            pltpu.VMEM((3, 2, 8, 128), f32),
            pltpu.VMEM((3, 8, 8, 128), f32),
            pltpu.VMEM((2, STEPS, 128), f32),
            pltpu.VMEM((6, GROUPS, 128), f32),
            pltpu.VMEM((GROUP_ROWS, 8, 128), f32),
            dma((5,)), dma((3, len(PIECES))),
            dma((3, len(PIECES1), 3)), dma((3, len(PIECES1), 3)),
            dma((3, len(PIECES), 3)), dma((3, len(PIECES), 3)),
            dma((3, len(PIECES), 7)), dma((3, len(PIECES), 7)),
            dma((3, 7)), dma((3, 7)),
            dma((4,)), dma((4,)),
        ],
        compiler_params=pltpu.CompilerParams(collective_id=0, has_side_effects=True, vmem_limit_bytes=48 << 20),
    )(
        *(pltpu.with_memory_space_constraint(a, pltpu.HBM) for a in (
        vel_base.reshape(256, 128), vel_grad.reshape(512, 128), route_dev.reshape(STEPS, GROUPS),
        route_block.reshape(STEPS, GROUPS), seed_cells)),
    )
    return pl.pallas_call(
        stretch_kernel,
        out_shape=(jax.ShapeDtypeStruct((2, 512, 128), f32), jax.ShapeDtypeStruct((512, 128), f32)),
        in_specs=[vmem] * 4,
        out_specs=(hbm, hbm),
        scratch_shapes=[pltpu.VMEM((2, 512, 128), f32), pltpu.VMEM((512, 128), f32), dma((2,))],
        compiler_params=pltpu.CompilerParams(vmem_limit_bytes=6 << 20),
    )(*moved)


def solution(mesh):
    in_specs = (
        P("lon", "lat", None, None, None, None),
        P("lon", "lat", None, None, None, None),
        P("lon", "lat", None, None, None),
        P("lon", "lat", None, None),
        P(None, "lat", "lon"),
    )
    out_specs = (P(None, "lat", "lon"), P("lat", "lon"))
    return jax.shard_map(body, mesh=mesh, in_specs=in_specs, out_specs=out_specs, check_vma=False)
```

```python
import jax
import jax.numpy as jnp
from jax import lax
from jax.experimental import pallas as pl
from jax.experimental.pallas import tpu as pltpu
from jax.sharding import PartitionSpec as P

MESH = pl.DeviceIdType.MESH
STEPS = 8
GROUPS = 128
GROUP_ROWS = 4
BLOCKS = 16
WIDTH = 256
DIMS = ((1, 2, 0), (2, 0, 1), (0, 1, 2))
PIECES1 = ((0, 2), (2, 6))
PIECES = ((0, 2), (2, 2), (4, 2), (6, 2))
NEAR = (1, 3, 2)
LINE = ((1, 0), (3, 0), (2, 0), (1, 1), (3, 1), (2, 1), (0, 1))


def owner_parts(owner):
    return (owner >> 5) & 3, (owner >> 3) & 3, owner & 3, (owner >> 2) & 1


def owner_number(place, core):
    return place[0] * 32 + place[1] * 8 + core * 4 + place[2]


def advect_kernel(
    base_hbm, grad_hbm, dev_hbm, block_hbm, cells_hbm, state, rows_in, cols_in, rows_out,
    base, grad, dev_ref, block_ref, cells, tab, rep, rcv, pick, sort, ask, asked, first, coef, edge_cells, edge, cols_out,
    load_sem, back_sem, send1, recv1, send2, recv2, send3, recv3, sendq, recvq, sendh, recvh,
):
    lon = lax.axis_index("lon")
    lat = lax.axis_index("lat")
    core = lon % 2
    here = (lon // 8, (lon // 2) % 4, lat)
    n_lon = 32

    def device(place, which):
        return ((place[0] * 4 + place[1]) * 2 + which, place[2])

    def moved(dim, by):
        place = list(here)
        place[dim] = (place[dim] + by) % 4
        return place

    east, west = (lon + 1) % n_lon, (lon + n_lon - 1) % n_lon
    partners = [device(moved(dim, by), (core + flip) % 2) for dim in range(3) for by in (1, 2, 3) for flip in (0, 1)]
    partners += [device(here, 1 - core), (east, lat), (west, lat)]
    barrier = pltpu.get_barrier_semaphore()
    for partner in partners:
        pl.semaphore_signal(barrier, inc=1, device_id=partner, device_id_type=MESH)

    loads = [
        pltpu.make_async_copy(src, dst, load_sem.at[i])
        for i, (src, dst) in enumerate(
            ((base_hbm, base), (grad_hbm, grad), (dev_hbm, dev_ref), (block_hbm, block_ref), (cells_hbm, cells))
        )
    ]
    for load in loads:
        load.start()

    row = lax.broadcasted_iota(jnp.int32, (256, 256), 0)
    column = lax.broadcasted_iota(jnp.int32, (256, 256), 1)
    order = jnp.where(column == (row & 127) * 2 + (row >> 7), 1.0, 0.0).astype(jnp.bfloat16)
    loads[0].wait()
    mine = jnp.dot(order, base[...], preferred_element_type=jnp.float32).astype(jnp.bfloat16)
    for m in range(2):
        part = mine[m * 128 : (m + 1) * 128].reshape(STEPS, BLOCKS, 128)
        tab[0, :, 0, 0, :, m * 128 : (m + 1) * 128] = part
    order = jnp.where(column == (row & 63) * 4 + (row >> 6), 1.0, 0.0).astype(jnp.bfloat16)
    loads[1].wait()
    for half in range(2):
        mine = jnp.dot(
            order, grad[half * 256 : (half + 1) * 256], preferred_element_type=jnp.float32
        ).astype(jnp.bfloat16)
        for m in range(4):
            k = 1 + m // 2
            part = mine[m * 64 : (m + 1) * 64].reshape(4, BLOCKS, 128)
            tab[k, half * 4 : half * 4 + 4, 0, 0, :, m % 2 * 128 : m % 2 * 128 + 128] = part
    pl.semaphore_wait(barrier, len(partners))

    def remote(src, dst, send, recv, target):
        return pltpu.make_async_remote_copy(
            src_ref=src, dst_ref=dst, send_sem=send, recv_sem=recv, device_id=target, device_id_type=MESH
        )

    phase1, early, phase2, phase3, query, back = {}, {}, {}, {}, {}, {}
    for k, (d1, d2, d3) in enumerate(DIMS):
        for c, (s0, n) in enumerate(PIECES1):
            steps = pl.ds(s0, n)
            for by in NEAR:
                phase1[k, c, by] = remote(
                    tab.at[k, steps, 0, 0], tab.at[k, steps, 0, by],
                    send1.at[k, c, by - 1], recv1.at[k, c, by - 1], device(moved(d1, by), core),
                )
                early[k, c, by] = remote(
                    tab.at[k, steps, 0, 0], tab.at[k, steps, by, 0],
                    send1.at[k, c, by + 2], recv1.at[k, c, by + 2], device(moved(d2, by), core),
                )
        slot = here[d3] * 2 + core
        for c, (s0, n) in enumerate(PIECES):
            for by in NEAR:
                phase2[k, c, by] = remote(
                    tab.at[k, pl.ds(s0, n), 0, pl.ds(1, 3)], tab.at[k, pl.ds(s0, n), by, pl.ds(1, 3)],
                    send2.at[k, c, by - 1], recv2.at[k, c, by - 1], device(moved(d2, by), core),
                )
            for i, (by, flip) in enumerate(LINE):
                place, which = moved(d3, by), (core + flip) % 2
                theirs = place[d3] * 2 + which
                phase3[k, c, i] = remote(
                    rep.at[k, pl.ds(s0, n), theirs], rcv.at[k, pl.ds(s0, n), slot],
                    send3.at[k, c, i], recv3.at[k, c, i], device(place, which),
                )
                if c == 0:
                    query[k, i] = remote(
                        ask.at[k, theirs // 4], asked.at[k, slot], sendq.at[k, i], recvq.at[k, i], device(place, which)
                    )
            back[k, c] = pltpu.make_async_copy(
                rep.at[k, pl.ds(s0, n), slot], rcv.at[k, pl.ds(s0, n), slot], back_sem.at[k, c]
            )

    for copies in (phase1, early):
        for c in range(len(PIECES1)):
            for by in NEAR:
                for k in range(3):
                    copies[k, c, by].start()

    loads[2].wait()
    loads[3].wait()
    lane = lax.broadcasted_iota(jnp.int32, (GROUPS, 128), 1)
    group = lax.broadcasted_iota(jnp.int32, (GROUPS, 128), 0)
    dev_columns = jnp.transpose(dev_ref[...].astype(jnp.float32))
    block_columns = jnp.transpose(block_ref[...].astype(jnp.float32))
    lane_f, group_f = lane.astype(jnp.float32), group.astype(jnp.float32)
    for s in range(STEPS):
        named = jnp.broadcast_to(dev_columns[:, s : s + 1], (GROUPS, 128)) == lane_f
        value = group_f * BLOCKS + jnp.broadcast_to(block_columns[:, s : s + 1], (GROUPS, 128))
        last = jnp.max(jnp.where(named, value, -1.0), axis=0, keepdims=True)
        least = jnp.min(jnp.where(named, value, 1e6), axis=0, keepdims=True)
        first[0, s : s + 1, :] = jnp.where(last >= 0.0, last - BLOCKS * jnp.floor(last * (1.0 / BLOCKS)), -1e4)
        first[1, s : s + 1, :] = jnp.where(least < last, least - BLOCKS * jnp.floor(least * (1.0 / BLOCKS)), -1e4)
    wide = lax.broadcasted_iota(jnp.int32, (8, 128), 1)
    for k, (d1, d2, d3) in enumerate(DIMS):
        for half in range(2):
            place = [None] * 3
            number = wide + half * 128
            place[d1], place[d2], place[d3] = (number >> 1) & 3, (number >> 3) & 3, (number >> 6) & 3
            index = owner_number(place, (number >> 5) & 1)
            chosen = jnp.where(
                (number & 1) == 0,
                jnp.take_along_axis(first[0], index, axis=1, mode="promise_in_bounds"),
                jnp.take_along_axis(first[1], index, axis=1, mode="promise_in_bounds"),
            )
            back_by = (((here[d2] - place[d2]) & 3) * 4 + ((here[d1] - place[d1]) & 3)) * BLOCKS
            ask[k, half] = chosen + back_by.astype(jnp.float32)
        for i in range(7):
            query[k, i].start()
        asked[k, here[d3] * 2 + core] = ask[k, here[d3] // 2]

    arrived = 0
    for c, (s0, n) in enumerate(PIECES):
        while arrived < len(PIECES1) and PIECES1[arrived][0] < s0 + n:
            for k in range(3):
                for by in NEAR:
                    phase1[k, arrived, by].wait_recv()
            arrived += 1
        for by in NEAR:
            for k in range(3):
                phase2[k, c, by].start()

    dev_int = dev_columns.astype(jnp.int32)
    slot_lane = lax.broadcasted_iota(jnp.int32, (GROUPS, WIDTH), 1)
    for s in range(STEPS):
        same = (jnp.broadcast_to(dev_columns[:, s : s + 1], (GROUPS, 128)) == dev_ref[s : s + 1, :].astype(jnp.float32)) & (
            lane > group
        )
        rank = jnp.max(jnp.where(same, 1.0, 0.0), axis=1, keepdims=True).astype(jnp.int32)
        x, y, z, which = owner_parts(dev_int[:, s : s + 1])
        place = (x, y, z)
        for k, (d1, d2, d3) in enumerate(DIMS):
            slot = (((place[d3] * 2 + which) * 4 + place[d2]) * 4 + place[d1]) * 2 + rank
            sort[k, s] = jnp.where(jnp.broadcast_to(slot, (GROUPS, WIDTH)) == slot_lane, -1.0 / STEPS, 0.0).astype(jnp.bfloat16)

    loads[4].wait()

    @pl.loop(0, STEPS)
    def _(step):
        packed = pltpu.roll(cells[step, pl.ds(0, GROUPS, stride=GROUP_ROWS), :], 1, 1)
        for q in range(1, GROUP_ROWS):
            turned = pltpu.roll(cells[step, pl.ds(q, GROUPS, stride=GROUP_ROWS), :], 2 * q + 1, 1)
            packed = jnp.where(lane // 2 == q, turned, packed)
        edge_cells[step] = packed

    state[...] = jnp.zeros_like(state)
    edge[...] = jnp.zeros_like(edge)

    block_lane = lax.broadcasted_iota(jnp.int32, (WIDTH, WIDTH), 1).astype(jnp.float32)
    for k, (_, _, d3) in enumerate(DIMS):
        for i in range(7):
            query[k, i].wait_recv()
        window = (here[d3] * 2 + core) % 4
        halves = []
        for half in range(2):
            total = jnp.full((8, 128), -1e4, jnp.float32)
            for r in range(4):
                turned = pltpu.roll(asked[k, half * 4 + r], (r - window + 4) % 4 * 32, 1)
                total = jnp.where(wide // 32 == r, turned, total)
            halves.append(jnp.transpose(total))
        rows = jnp.concatenate(halves, axis=0)
        for s in range(STEPS):
            pick[k, s] = jnp.where(
                jnp.broadcast_to(rows[:, s : s + 1], (WIDTH, WIDTH)) == block_lane, 1.0, 0.0
            ).astype(jnp.bfloat16)

    arrived = 0
    for c, (s0, n) in enumerate(PIECES):
        while arrived < len(PIECES1) and PIECES1[arrived][0] < s0 + n:
            for k in range(3):
                for by in NEAR:
                    early[k, arrived, by].wait_recv()
            arrived += 1
        for k in range(3):
            for by in NEAR:
                phase2[k, c, by].wait_recv()
            for s in range(s0, s0 + n):
                found = jnp.dot(pick[k, s], tab[k, s].reshape(WIDTH, WIDTH), preferred_element_type=jnp.float32)
                rep[k, s] = found.astype(jnp.bfloat16).reshape(8, 32, WIDTH)
            for i in range(7):
                phase3[k, c, i].start()
            back[k, c].start()

    def collect(c):
        for k in range(3):
            back[k, c].wait()
            for i in range(7):
                phase3[k, c, i].wait_recv()

    def sort_blocks(step, at):
        for k in range(3):
            found = jnp.dot(sort[k, step], rcv[k, step].reshape(WIDTH, WIDTH), preferred_element_type=jnp.float32)
            coef[at, 2 * k] = found[:, :128]
            coef[at, 2 * k + 1] = found[:, 128:]

    def advance(at, start, index, px, py):
        vx, vy, gxx, gxy, gyx, gyy = (
            jnp.take_along_axis(coef[at, m, start : start + 8, :], index, axis=1, mode="promise_in_bounds")
            for m in range(6)
        )
        kx = vx + (gxx * px + gxy * py)
        ky = vy + (gyx * px + gyy * py)
        wx, wy = kx, ky
        for part in (0.25, 1.0 / 3.0, 0.5):
            wx, wy = kx + part * (gxx * wx + gxy * wy), ky + part * (gyx * wx + gyy * wy)
        return px + wx, py + wy

    def advance_edge(start, steps):
        rows = slice(start, start + 8)
        px, py = edge[0, rows, :], edge[1, rows, :]
        for at, step in steps:
            px, py = advance(at, start, edge_cells[step, rows, :], px, py)
        edge[0, rows, :], edge[1, rows, :] = px, py

    def advance_rows(start, steps):
        rows = slice(start, start + 8)
        for q in range(GROUP_ROWS):
            px, py = state[0, q, rows, :], state[1, q, rows, :]
            for at, step in steps:
                index = cells[step, pl.ds(start * GROUP_ROWS + q, 8, stride=GROUP_ROWS), :]
                px, py = advance(at, start, index, px, py)
            state[0, q, rows, :], state[1, q, rows, :] = px, py

    for c, (s0, n) in enumerate(PIECES[:-1]):
        collect(c)

        @pl.loop(s0, s0 + n)
        def _(step):
            sort_blocks(step, 0)
            for start in range(0, GROUPS, 8):
                advance_edge(start, [(0, step)])
                advance_rows(start, [(0, step)])

    s0, n = PIECES[-1]
    collect(len(PIECES) - 1)
    steps = [(i, s0 + i) for i in range(n)]
    for at, step in steps:
        sort_blocks(step, at)
    for start in range(0, GROUPS, 8):
        advance_edge(start, steps)
    for comp in range(2):
        cols_out[comp] = jnp.transpose(edge[comp])[:8, :]
    halo = []
    for i, lon_to in enumerate((east, west)):
        halo.append(remote(cols_out, cols_in.at[i], sendh.at[i], recvh.at[i], (lon_to, lat)))
        halo[-1].start()
    for start in (0, GROUPS - 8):
        advance_rows(start, steps)
    rows_out[...] = jnp.zeros_like(rows_out)
    for comp in range(2):
        rows_out[comp : comp + 1, :] = state[comp, 0, 0:1, :]
        rows_out[2 + comp : 3 + comp, :] = state[comp, GROUP_ROWS - 1, GROUPS - 1 : GROUPS, :]
    for i, by in enumerate((1, 3)):
        halo.append(remote(rows_out, rows_in.at[i], sendh.at[2 + i], recvh.at[2 + i], device(moved(2, by), core)))
        halo[-1].start()
    for start in range(8, GROUPS - 8, 8):
        advance_rows(start, steps)
    for copies in (phase1, early, phase2, phase3, query):
        for copy in copies.values():
            copy.wait_send()
    for copy in halo:
        copy.wait_send()
        copy.wait_recv()


def stretch_kernel(state, rows_in, cols_in, rows_out, flow_hbm, ftle_hbm, flow, ftle, sem):
    lat = lax.axis_index("lat")
    for comp in range(2):
        for q in range(GROUP_ROWS):
            flow[comp, pl.ds(q, GROUPS, stride=GROUP_ROWS), :] = state[comp, q]
    flow_copy = pltpu.make_async_copy(flow, flow_hbm, sem.at[0])
    flow_copy.start()
    lane = lax.broadcasted_iota(jnp.int32, (GROUPS, 128), 1)
    group = lax.broadcasted_iota(jnp.int32, (GROUPS, 128), 0)
    south_own, north_own = lat == 0, lat == 3
    at_west, at_east = lane == 0, lane == 127
    bottom, top = group == 0, group == GROUPS - 1
    diffs = {}
    for comp in range(2):
        south = jnp.where(south_own, rows_out[comp : comp + 1, :], rows_in[0, 2 + comp : 3 + comp, :])
        north = jnp.where(north_own, rows_out[2 + comp : 3 + comp, :], rows_in[1, comp : comp + 1, :])
        from_west, from_east = jnp.transpose(cols_in[0, comp]), jnp.transpose(cols_in[1, comp])
        for q in range(GROUP_ROWS):
            own_rows = state[comp, q]
            west_column = from_west[:, 2 * q : 2 * q + 1]
            east_column = from_east[:, 2 * q + 1 : 2 * q + 2]
            low = jnp.where(at_west, west_column, pltpu.roll(own_rows, 1, 1))
            high = jnp.where(at_east, east_column, pltpu.roll(own_rows, 127, 1))
            diffs[comp, q, 0] = (high - low) * 0.5
            if q == 0:
                below = jnp.where(bottom, south, pltpu.roll(state[comp, GROUP_ROWS - 1], 1, 0))
            else:
                below = state[comp, q - 1]
            if q == GROUP_ROWS - 1:
                above = jnp.where(top, north, pltpu.roll(state[comp, 0], GROUPS - 1, 0))
            else:
                above = state[comp, q + 1]
            diffs[comp, q, 1] = (above - below) * 0.5
    for q in range(GROUP_ROWS):
        map_xx, map_yx = 1.0 + diffs[0, q, 0], diffs[1, q, 0]
        map_xy, map_yy = diffs[0, q, 1], 1.0 + diffs[1, q, 1]
        green_xx = map_xx * map_xx + map_yx * map_yx
        green_yy = map_xy * map_xy + map_yy * map_yy
        green_xy = map_xx * map_xy + map_yx * map_yy
        half_diff = 0.5 * (green_xx - green_yy)
        largest = 0.5 * (green_xx + green_yy) + jnp.sqrt(half_diff * half_diff + green_xy * green_xy)
        ftle[pl.ds(q, GROUPS, stride=GROUP_ROWS), :] = 0.5 * jnp.log(largest)
    ftle_copy = pltpu.make_async_copy(ftle, ftle_hbm, sem.at[1])
    ftle_copy.start()
    flow_copy.wait()
    ftle_copy.wait()


def body(vel_base, vel_grad, route_dev, route_block, seed_cells):
    dma = pltpu.SemaphoreType.DMA
    vmem = pl.BlockSpec(memory_space=pltpu.VMEM)
    hbm = pl.BlockSpec(memory_space=pltpu.HBM)
    bf16, f32, i32 = jnp.bfloat16, jnp.float32, jnp.int32
    moved = pl.pallas_call(
        advect_kernel,
        out_shape=(
            jax.ShapeDtypeStruct((2, GROUP_ROWS, GROUPS, 128), f32),
            jax.ShapeDtypeStruct((2, 8, 128), f32),
            jax.ShapeDtypeStruct((2, 2, 8, 128), f32),
            jax.ShapeDtypeStruct((8, 128), f32),
        ),
        in_specs=[hbm] * 5,
        out_specs=(vmem,) * 4,
        scratch_shapes=[
            pltpu.VMEM((256, 128), bf16),
            pltpu.VMEM((512, 128), bf16),
            pltpu.VMEM((STEPS, GROUPS), i32),
            pltpu.VMEM((STEPS, GROUPS), i32),
            pltpu.VMEM((STEPS, 512, 128), i32),
            pltpu.VMEM((3, STEPS, 4, 4, BLOCKS, WIDTH), bf16),
            pltpu.VMEM((3, STEPS, 8, 32, WIDTH), bf16),
            pltpu.VMEM((3, STEPS, 8, 32, WIDTH), bf16),
            pltpu.VMEM((3, STEPS, WIDTH, WIDTH), bf16),
            pltpu.VMEM((3, STEPS, GROUPS, WIDTH), bf16),
            pltpu.VMEM((3, 2, 8, 128), f32),
            pltpu.VMEM((3, 8, 8, 128), f32),
            pltpu.VMEM((2, STEPS, 128), f32),
            pltpu.VMEM((PIECES[-1][1], 6, GROUPS, 128), f32),
            pltpu.VMEM((STEPS, GROUPS, 128), i32),
            pltpu.VMEM((2, GROUPS, 128), f32),
            pltpu.VMEM((2, 8, 128), f32),
            dma((5,)), dma((3, len(PIECES))),
            dma((3, len(PIECES1), 6)), dma((3, len(PIECES1), 6)),
            dma((3, len(PIECES), 3)), dma((3, len(PIECES), 3)),
            dma((3, len(PIECES), 7)), dma((3, len(PIECES), 7)),
            dma((3, 7)), dma((3, 7)),
            dma((4,)), dma((4,)),
        ],
        compiler_params=pltpu.CompilerParams(collective_id=0, has_side_effects=True, vmem_limit_bytes=48 << 20),
    )(
        *(pltpu.with_memory_space_constraint(a, pltpu.HBM) for a in (
        vel_base.reshape(256, 128), vel_grad.reshape(512, 128), route_dev.reshape(STEPS, GROUPS),
        route_block.reshape(STEPS, GROUPS), seed_cells)),
    )
    return pl.pallas_call(
        stretch_kernel,
        out_shape=(jax.ShapeDtypeStruct((2, 512, 128), f32), jax.ShapeDtypeStruct((512, 128), f32)),
        in_specs=[vmem] * 4,
        out_specs=(hbm, hbm),
        scratch_shapes=[pltpu.VMEM((2, 512, 128), f32), pltpu.VMEM((512, 128), f32), dma((2,))],
        compiler_params=pltpu.CompilerParams(vmem_limit_bytes=6 << 20),
    )(*moved)


def solution(mesh):
    in_specs = (
        P("lon", "lat", None, None, None, None),
        P("lon", "lat", None, None, None, None),
        P("lon", "lat", None, None, None),
        P("lon", "lat", None, None),
        P(None, "lat", "lon"),
    )
    out_specs = (P(None, "lat", "lon"), P("lat", "lon"))
    return jax.shard_map(body, mesh=mesh, in_specs=in_specs, out_specs=out_specs, check_vma=False)
```

```python
import jax
import jax.numpy as jnp
from jax import lax
from jax.experimental import pallas as pl
from jax.experimental.pallas import tpu as pltpu
from jax.sharding import PartitionSpec as P

MESH = pl.DeviceIdType.MESH
STEPS = 8
GROUPS = 128
GROUP_ROWS = 4
BLOCKS = 16
WIDTH = 256
DIMS = ((1, 2, 0), (2, 0, 1), (0, 1, 2))
PIECES1 = ((0, 8),)
PIECES2 = ((0, 4), (4, 4))
PIECES = ((0, 4), (4, 4))
NEAR = (1, 3, 2)
LINE = ((1, 0), (3, 0), (2, 0), (1, 1), (3, 1), (2, 1), (0, 1))


def owner_parts(owner):
    return (owner >> 5) & 3, (owner >> 3) & 3, owner & 3, (owner >> 2) & 1


def owner_number(place, core):
    return place[0] * 32 + place[1] * 8 + core * 4 + place[2]


def advect_kernel(
    base_hbm, grad_hbm, dev_hbm, block_hbm, cells_hbm, state, rows_in, cols_in, rows_out,
    base, grad, dev_ref, block_ref, cells, tab, rep, rcv, pick, sort, ask, asked, first, coef, edge_cells, edge, cols_out,
    load_sem, back_sem, send1, recv1, send2, recv2, send3, recv3, sendq, recvq, sendh, recvh,
):
    lon = lax.axis_index("lon")
    lat = lax.axis_index("lat")
    core = lon % 2
    here = (lon // 8, (lon // 2) % 4, lat)
    n_lon = 32

    def device(place, which):
        return ((place[0] * 4 + place[1]) * 2 + which, place[2])

    def moved(dim, by):
        place = list(here)
        place[dim] = (place[dim] + by) % 4
        return place

    east, west = (lon + 1) % n_lon, (lon + n_lon - 1) % n_lon
    partners = [device(moved(dim, by), (core + flip) % 2) for dim in range(3) for by in (1, 2, 3) for flip in (0, 1)]
    partners += [device(here, 1 - core), (east, lat), (west, lat)]
    barrier = pltpu.get_barrier_semaphore()
    for partner in partners:
        pl.semaphore_signal(barrier, inc=1, device_id=partner, device_id_type=MESH)

    loads = [
        pltpu.make_async_copy(src, dst, load_sem.at[i])
        for i, (src, dst) in enumerate(
            ((base_hbm, base), (grad_hbm, grad), (dev_hbm, dev_ref), (block_hbm, block_ref), (cells_hbm, cells))
        )
    ]
    for load in loads:
        load.start()

    row = lax.broadcasted_iota(jnp.int32, (256, 256), 0)
    column = lax.broadcasted_iota(jnp.int32, (256, 256), 1)
    order = jnp.where(column == (row & 127) * 2 + (row >> 7), 1.0, 0.0).astype(jnp.bfloat16)
    loads[0].wait()
    mine = jnp.dot(order, base[...], preferred_element_type=jnp.float32).astype(jnp.bfloat16)
    for m in range(2):
        part = mine[m * 128 : (m + 1) * 128].reshape(STEPS, BLOCKS, 128)
        tab[0, :, 0, 0, :, m * 128 : (m + 1) * 128] = part
    order = jnp.where(column == (row & 63) * 4 + (row >> 6), 1.0, 0.0).astype(jnp.bfloat16)
    loads[1].wait()
    for half in range(2):
        mine = jnp.dot(
            order, grad[half * 256 : (half + 1) * 256], preferred_element_type=jnp.float32
        ).astype(jnp.bfloat16)
        for m in range(4):
            k = 1 + m // 2
            part = mine[m * 64 : (m + 1) * 64].reshape(4, BLOCKS, 128)
            tab[k, half * 4 : half * 4 + 4, 0, 0, :, m % 2 * 128 : m % 2 * 128 + 128] = part
    pl.semaphore_wait(barrier, len(partners))

    def remote(src, dst, send, recv, target):
        return pltpu.make_async_remote_copy(
            src_ref=src, dst_ref=dst, send_sem=send, recv_sem=recv, device_id=target, device_id_type=MESH
        )

    phase1, early, phase2, phase3, query, back = {}, {}, {}, {}, {}, {}
    for k, (d1, d2, d3) in enumerate(DIMS):
        for c, (s0, n) in enumerate(PIECES1):
            steps = pl.ds(s0, n)
            for by in NEAR:
                phase1[k, c, by] = remote(
                    tab.at[k, steps, 0, 0], tab.at[k, steps, 0, by],
                    send1.at[k, c, by - 1], recv1.at[k, c, by - 1], device(moved(d1, by), core),
                )
                early[k, c, by] = remote(
                    tab.at[k, steps, 0, 0], tab.at[k, steps, by, 0],
                    send1.at[k, c, by + 2], recv1.at[k, c, by + 2], device(moved(d2, by), core),
                )
        slot = here[d3] * 2 + core
        for c, (s0, n) in enumerate(PIECES2):
            for by in NEAR:
                phase2[k, c, by] = remote(
                    tab.at[k, pl.ds(s0, n), 0, pl.ds(1, 3)], tab.at[k, pl.ds(s0, n), by, pl.ds(1, 3)],
                    send2.at[k, c, by - 1], recv2.at[k, c, by - 1], device(moved(d2, by), core),
                )
        for c, (s0, n) in enumerate(PIECES):
            for i, (by, flip) in enumerate(LINE):
                place, which = moved(d3, by), (core + flip) % 2
                theirs = place[d3] * 2 + which
                phase3[k, c, i] = remote(
                    rep.at[k, theirs, pl.ds(s0, n)], rcv.at[k, slot, pl.ds(s0, n)],
                    send3.at[k, c, i], recv3.at[k, c, i], device(place, which),
                )
                if c == 0:
                    query[k, i] = remote(
                        ask.at[k, theirs // 4], asked.at[k, slot], sendq.at[k, i], recvq.at[k, i], device(place, which)
                    )
            back[k, c] = pltpu.make_async_copy(
                rep.at[k, slot, pl.ds(s0, n)], rcv.at[k, slot, pl.ds(s0, n)], back_sem.at[k, c]
            )

    for copies in (phase1, early):
        for c in range(len(PIECES1)):
            for by in NEAR:
                for k in range(3):
                    copies[k, c, by].start()

    loads[2].wait()
    loads[3].wait()
    lane = lax.broadcasted_iota(jnp.int32, (GROUPS, 128), 1)
    group = lax.broadcasted_iota(jnp.int32, (GROUPS, 128), 0)
    dev_columns = jnp.transpose(dev_ref[...].astype(jnp.float32))
    block_columns = jnp.transpose(block_ref[...].astype(jnp.float32))
    lane_f, group_f = lane.astype(jnp.float32), group.astype(jnp.float32)
    for s in range(STEPS):
        named = jnp.broadcast_to(dev_columns[:, s : s + 1], (GROUPS, 128)) == lane_f
        value = group_f * BLOCKS + jnp.broadcast_to(block_columns[:, s : s + 1], (GROUPS, 128))
        last = jnp.max(jnp.where(named, value, -1.0), axis=0, keepdims=True)
        least = jnp.min(jnp.where(named, value, 1e6), axis=0, keepdims=True)
        first[0, s : s + 1, :] = jnp.where(last >= 0.0, last - BLOCKS * jnp.floor(last * (1.0 / BLOCKS)), -1e4)
        first[1, s : s + 1, :] = jnp.where(least < last, least - BLOCKS * jnp.floor(least * (1.0 / BLOCKS)), -1e4)
    wide = lax.broadcasted_iota(jnp.int32, (8, 128), 1)
    for k, (d1, d2, d3) in enumerate(DIMS):
        for half in range(2):
            place = [None] * 3
            number = wide + half * 128
            place[d1], place[d2], place[d3] = (number >> 1) & 3, (number >> 3) & 3, (number >> 6) & 3
            index = owner_number(place, (number >> 5) & 1)
            chosen = jnp.where(
                (number & 1) == 0,
                jnp.take_along_axis(first[0], index, axis=1, mode="promise_in_bounds"),
                jnp.take_along_axis(first[1], index, axis=1, mode="promise_in_bounds"),
            )
            back_by = (((here[d2] - place[d2]) & 3) * 4 + ((here[d1] - place[d1]) & 3)) * BLOCKS
            ask[k, half] = chosen + back_by.astype(jnp.float32)
        for i in range(7):
            query[k, i].start()
        asked[k, here[d3] * 2 + core] = ask[k, here[d3] // 2]

    arrived = 0
    for c, (s0, n) in enumerate(PIECES2):
        while arrived < len(PIECES1) and PIECES1[arrived][0] < s0 + n:
            for k in range(3):
                for by in NEAR:
                    phase1[k, arrived, by].wait_recv()
            arrived += 1
        for by in NEAR:
            for k in range(3):
                phase2[k, c, by].start()

    dev_int = dev_columns.astype(jnp.int32)
    slot_lane = lax.broadcasted_iota(jnp.int32, (GROUPS, WIDTH), 1)
    for s in range(STEPS):
        same = (jnp.broadcast_to(dev_columns[:, s : s + 1], (GROUPS, 128)) == dev_ref[s : s + 1, :].astype(jnp.float32)) & (
            lane > group
        )
        rank = jnp.max(jnp.where(same, 1.0, 0.0), axis=1, keepdims=True).astype(jnp.int32)
        x, y, z, which = owner_parts(dev_int[:, s : s + 1])
        place = (x, y, z)
        for k, (d1, d2, d3) in enumerate(DIMS):
            slot = (((place[d3] * 2 + which) * 4 + place[d2]) * 4 + place[d1]) * 2 + rank
            sort[k, s] = jnp.where(jnp.broadcast_to(slot, (GROUPS, WIDTH)) == slot_lane, -1.0 / STEPS, 0.0).astype(jnp.bfloat16)

    loads[4].wait()

    @pl.loop(0, STEPS)
    def _(step):
        packed = pltpu.roll(cells[step, pl.ds(0, GROUPS, stride=GROUP_ROWS), :], 1, 1)
        for q in range(1, GROUP_ROWS):
            turned = pltpu.roll(cells[step, pl.ds(q, GROUPS, stride=GROUP_ROWS), :], 2 * q + 1, 1)
            packed = jnp.where(lane // 2 == q, turned, packed)
        edge_cells[step] = packed

    state[...] = jnp.zeros_like(state)
    edge[...] = jnp.zeros_like(edge)

    block_lane = lax.broadcasted_iota(jnp.int32, (WIDTH, WIDTH), 1).astype(jnp.float32)
    for k, (_, _, d3) in enumerate(DIMS):
        for i in range(7):
            query[k, i].wait_recv()
        window = (here[d3] * 2 + core) % 4
        halves = []
        for half in range(2):
            total = jnp.full((8, 128), -1e4, jnp.float32)
            for r in range(4):
                turned = pltpu.roll(asked[k, half * 4 + r], (r - window + 4) % 4 * 32, 1)
                total = jnp.where(wide // 32 == r, turned, total)
            halves.append(jnp.transpose(total))
        rows = jnp.concatenate(halves, axis=0)
        for s in range(STEPS):
            pick[k, s] = jnp.where(
                jnp.broadcast_to(rows[:, s : s + 1], (WIDTH, WIDTH)) == block_lane, 1.0, 0.0
            ).astype(jnp.bfloat16)

    arrived = sent = 0
    for c, (s0, n) in enumerate(PIECES2):
        while arrived < len(PIECES1) and PIECES1[arrived][0] < s0 + n:
            for k in range(3):
                for by in NEAR:
                    early[k, arrived, by].wait_recv()
            arrived += 1
        for k in range(3):
            for by in NEAR:
                phase2[k, c, by].wait_recv()
        while sent < len(PIECES) and sum(PIECES[sent]) <= s0 + n:
            for k in range(3):
                for s in range(PIECES[sent][0], sum(PIECES[sent])):
                    found = jnp.dot(pick[k, s], tab[k, s].reshape(WIDTH, WIDTH), preferred_element_type=jnp.float32)
                    rep[k, :, s] = found.astype(jnp.bfloat16).reshape(8, 32, WIDTH)
                for i in range(7):
                    phase3[k, sent, i].start()
                back[k, sent].start()
            sent += 1

    def collect(c):
        for k in range(3):
            back[k, c].wait()
            for i in range(7):
                phase3[k, c, i].wait_recv()

    def sort_blocks(step, at):
        for k in range(3):
            found = jnp.dot(sort[k, step], rcv[k, :, step].reshape(WIDTH, WIDTH), preferred_element_type=jnp.float32)
            coef[at, 2 * k] = found[:, :128]
            coef[at, 2 * k + 1] = found[:, 128:]

    def advance(at, start, index, px, py):
        vx, vy, gxx, gxy, gyx, gyy = (
            jnp.take_along_axis(coef[at, m, start : start + 8, :], index, axis=1, mode="promise_in_bounds")
            for m in range(6)
        )
        kx = vx + (gxx * px + gxy * py)
        ky = vy + (gyx * px + gyy * py)
        wx, wy = kx, ky
        for part in (0.25, 1.0 / 3.0, 0.5):
            wx, wy = kx + part * (gxx * wx + gxy * wy), ky + part * (gyx * wx + gyy * wy)
        return px + wx, py + wy

    def advance_edge(start, steps):
        rows = slice(start, start + 8)
        px, py = edge[0, rows, :], edge[1, rows, :]
        for at, step in steps:
            px, py = advance(at, start, edge_cells[step, rows, :], px, py)
        edge[0, rows, :], edge[1, rows, :] = px, py

    def advance_rows(start, steps):
        rows = slice(start, start + 8)
        for q in range(GROUP_ROWS):
            px, py = state[0, q, rows, :], state[1, q, rows, :]
            for at, step in steps:
                index = cells[step, pl.ds(start * GROUP_ROWS + q, 8, stride=GROUP_ROWS), :]
                px, py = advance(at, start, index, px, py)
            state[0, q, rows, :], state[1, q, rows, :] = px, py

    for c, (s0, n) in enumerate(PIECES[:-1]):
        collect(c)

        @pl.loop(s0, s0 + n)
        def _(step):
            sort_blocks(step, 0)
            for start in range(0, GROUPS, 8):
                advance_edge(start, [(0, step)])
                advance_rows(start, [(0, step)])

    s0, n = PIECES[-1]
    collect(len(PIECES) - 1)
    steps = [(i, s0 + i) for i in range(n)]
    for at, step in steps:
        sort_blocks(step, at)
    for start in range(0, GROUPS, 8):
        advance_edge(start, steps)
    for comp in range(2):
        cols_out[comp] = jnp.transpose(edge[comp])[:8, :]
    halo = []
    for i, lon_to in enumerate((east, west)):
        halo.append(remote(cols_out, cols_in.at[i], sendh.at[i], recvh.at[i], (lon_to, lat)))
        halo[-1].start()
    for start in (0, GROUPS - 8):
        advance_rows(start, steps)
    rows_out[...] = jnp.zeros_like(rows_out)
    for comp in range(2):
        rows_out[comp : comp + 1, :] = state[comp, 0, 0:1, :]
        rows_out[2 + comp : 3 + comp, :] = state[comp, GROUP_ROWS - 1, GROUPS - 1 : GROUPS, :]
    for i, by in enumerate((1, 3)):
        halo.append(remote(rows_out, rows_in.at[i], sendh.at[2 + i], recvh.at[2 + i], device(moved(2, by), core)))
        halo[-1].start()
    for start in range(8, GROUPS - 8, 8):
        advance_rows(start, steps)
    for copies in (phase1, early, phase2, phase3, query):
        for copy in copies.values():
            copy.wait_send()
    for copy in halo:
        copy.wait_send()
        copy.wait_recv()


def stretch_kernel(state, rows_in, cols_in, rows_out, flow_hbm, ftle_hbm, flow, ftle, sem):
    lat = lax.axis_index("lat")
    for comp in range(2):
        for q in range(GROUP_ROWS):
            flow[comp, pl.ds(q, GROUPS, stride=GROUP_ROWS), :] = state[comp, q]
    flow_copy = pltpu.make_async_copy(flow, flow_hbm, sem.at[0])
    flow_copy.start()
    lane = lax.broadcasted_iota(jnp.int32, (GROUPS, 128), 1)
    group = lax.broadcasted_iota(jnp.int32, (GROUPS, 128), 0)
    south_own, north_own = lat == 0, lat == 3
    at_west, at_east = lane == 0, lane == 127
    bottom, top = group == 0, group == GROUPS - 1
    diffs = {}
    for comp in range(2):
        south = jnp.where(south_own, rows_out[comp : comp + 1, :], rows_in[0, 2 + comp : 3 + comp, :])
        north = jnp.where(north_own, rows_out[2 + comp : 3 + comp, :], rows_in[1, comp : comp + 1, :])
        from_west, from_east = jnp.transpose(cols_in[0, comp]), jnp.transpose(cols_in[1, comp])
        for q in range(GROUP_ROWS):
            own_rows = state[comp, q]
            west_column = from_west[:, 2 * q : 2 * q + 1]
            east_column = from_east[:, 2 * q + 1 : 2 * q + 2]
            low = jnp.where(at_west, west_column, pltpu.roll(own_rows, 1, 1))
            high = jnp.where(at_east, east_column, pltpu.roll(own_rows, 127, 1))
            diffs[comp, q, 0] = (high - low) * 0.5
            if q == 0:
                below = jnp.where(bottom, south, pltpu.roll(state[comp, GROUP_ROWS - 1], 1, 0))
            else:
                below = state[comp, q - 1]
            if q == GROUP_ROWS - 1:
                above = jnp.where(top, north, pltpu.roll(state[comp, 0], GROUPS - 1, 0))
            else:
                above = state[comp, q + 1]
            diffs[comp, q, 1] = (above - below) * 0.5
    for q in range(GROUP_ROWS):
        map_xx, map_yx = 1.0 + diffs[0, q, 0], diffs[1, q, 0]
        map_xy, map_yy = diffs[0, q, 1], 1.0 + diffs[1, q, 1]
        green_xx = map_xx * map_xx + map_yx * map_yx
        green_yy = map_xy * map_xy + map_yy * map_yy
        green_xy = map_xx * map_xy + map_yx * map_yy
        half_diff = 0.5 * (green_xx - green_yy)
        largest = 0.5 * (green_xx + green_yy) + jnp.sqrt(half_diff * half_diff + green_xy * green_xy)
        ftle[pl.ds(q, GROUPS, stride=GROUP_ROWS), :] = 0.5 * jnp.log(largest)
    ftle_copy = pltpu.make_async_copy(ftle, ftle_hbm, sem.at[1])
    ftle_copy.start()
    flow_copy.wait()
    ftle_copy.wait()


def body(vel_base, vel_grad, route_dev, route_block, seed_cells):
    dma = pltpu.SemaphoreType.DMA
    vmem = pl.BlockSpec(memory_space=pltpu.VMEM)
    hbm = pl.BlockSpec(memory_space=pltpu.HBM)
    bf16, f32, i32 = jnp.bfloat16, jnp.float32, jnp.int32
    moved = pl.pallas_call(
        advect_kernel,
        out_shape=(
            jax.ShapeDtypeStruct((2, GROUP_ROWS, GROUPS, 128), f32),
            jax.ShapeDtypeStruct((2, 8, 128), f32),
            jax.ShapeDtypeStruct((2, 2, 8, 128), f32),
            jax.ShapeDtypeStruct((8, 128), f32),
        ),
        in_specs=[hbm] * 5,
        out_specs=(vmem,) * 4,
        scratch_shapes=[
            pltpu.VMEM((256, 128), bf16),
            pltpu.VMEM((512, 128), bf16),
            pltpu.VMEM((STEPS, GROUPS), i32),
            pltpu.VMEM((STEPS, GROUPS), i32),
            pltpu.VMEM((STEPS, 512, 128), i32),
            pltpu.VMEM((3, STEPS, 4, 4, BLOCKS, WIDTH), bf16),
            pltpu.VMEM((3, STEPS, 8, 32, WIDTH), bf16),
            pltpu.VMEM((3, STEPS, 8, 32, WIDTH), bf16),
            pltpu.VMEM((3, STEPS, WIDTH, WIDTH), bf16),
            pltpu.VMEM((3, STEPS, GROUPS, WIDTH), bf16),
            pltpu.VMEM((3, 2, 8, 128), f32),
            pltpu.VMEM((3, 8, 8, 128), f32),
            pltpu.VMEM((2, STEPS, 128), f32),
            pltpu.VMEM((PIECES[-1][1], 6, GROUPS, 128), f32),
            pltpu.VMEM((STEPS, GROUPS, 128), i32),
            pltpu.VMEM((2, GROUPS, 128), f32),
            pltpu.VMEM((2, 8, 128), f32),
            dma((5,)), dma((3, len(PIECES))),
            dma((3, len(PIECES1), 6)), dma((3, len(PIECES1), 6)),
            dma((3, len(PIECES2), 3)), dma((3, len(PIECES2), 3)),
            dma((3, len(PIECES), 7)), dma((3, len(PIECES), 7)),
            dma((3, 7)), dma((3, 7)),
            dma((4,)), dma((4,)),
        ],
        compiler_params=pltpu.CompilerParams(collective_id=0, has_side_effects=True, vmem_limit_bytes=48 << 20),
    )(
        *(pltpu.with_memory_space_constraint(a, pltpu.HBM) for a in (
        vel_base.reshape(256, 128), vel_grad.reshape(512, 128), route_dev.reshape(STEPS, GROUPS),
        route_block.reshape(STEPS, GROUPS), seed_cells)),
    )
    return pl.pallas_call(
        stretch_kernel,
        out_shape=(jax.ShapeDtypeStruct((2, 512, 128), f32), jax.ShapeDtypeStruct((512, 128), f32)),
        in_specs=[vmem] * 4,
        out_specs=(hbm, hbm),
        scratch_shapes=[pltpu.VMEM((2, 512, 128), f32), pltpu.VMEM((512, 128), f32), dma((2,))],
        compiler_params=pltpu.CompilerParams(vmem_limit_bytes=6 << 20),
    )(*moved)


def solution(mesh):
    in_specs = (
        P("lon", "lat", None, None, None, None),
        P("lon", "lat", None, None, None, None),
        P("lon", "lat", None, None, None),
        P("lon", "lat", None, None),
        P(None, "lat", "lon"),
    )
    out_specs = (P(None, "lat", "lon"), P("lat", "lon"))
    return jax.shard_map(body, mesh=mesh, in_specs=in_specs, out_specs=out_specs, check_vma=False)
```

```python
import jax
import jax.numpy as jnp
from jax import lax
from jax.experimental import pallas as pl
from jax.experimental.pallas import tpu as pltpu
from jax.sharding import PartitionSpec as P

MESH = pl.DeviceIdType.MESH
STEPS = 8
GROUPS = 128
GROUP_ROWS = 4
BLOCKS = 16
WIDTH = 256
DIMS = ((1, 2, 0), (2, 0, 1), (0, 1, 2))
PIECES1 = ((0, 8),)
PIECES2 = ((0, 4), (4, 4))
PIECES = ((0, 4), (4, 4))
NEAR = (1, 3, 2)
LINE = ((1, 0), (3, 0), (2, 0), (1, 1), (3, 1), (2, 1), (0, 1))


def owner_parts(owner):
    return (owner >> 5) & 3, (owner >> 3) & 3, owner & 3, (owner >> 2) & 1


def owner_number(place, core):
    return place[0] * 32 + place[1] * 8 + core * 4 + place[2]


def advect_kernel(
    base_hbm, grad_hbm, dev_hbm, block_hbm, cells_hbm, state, rows_in, cols_in, rows_out, flow,
    base, grad, dev_ref, block_ref, cells, tab, rep, rcv, pick, sort, ask, asked, first, coef, edge_cells, edge, cols_out,
    load_sem, back_sem, send1, recv1, send2, recv2, send3, recv3, sendq, recvq, sendh, recvh,
):
    lon = lax.axis_index("lon")
    lat = lax.axis_index("lat")
    core = lon % 2
    here = (lon // 8, (lon // 2) % 4, lat)
    n_lon = 32

    def device(place, which):
        return ((place[0] * 4 + place[1]) * 2 + which, place[2])

    def moved(dim, by):
        place = list(here)
        place[dim] = (place[dim] + by) % 4
        return place

    east, west = (lon + 1) % n_lon, (lon + n_lon - 1) % n_lon
    partners = [device(moved(dim, by), (core + flip) % 2) for dim in range(3) for by in (1, 2, 3) for flip in (0, 1)]
    partners += [device(here, 1 - core), (east, lat), (west, lat)]
    barrier = pltpu.get_barrier_semaphore()
    for partner in partners:
        pl.semaphore_signal(barrier, inc=1, device_id=partner, device_id_type=MESH)

    loads = [
        pltpu.make_async_copy(src, dst, load_sem.at[i])
        for i, (src, dst) in enumerate(
            ((base_hbm, base), (grad_hbm, grad), (dev_hbm, dev_ref), (block_hbm, block_ref), (cells_hbm, cells))
        )
    ]
    for load in loads:
        load.start()

    row = lax.broadcasted_iota(jnp.int32, (256, 256), 0)
    column = lax.broadcasted_iota(jnp.int32, (256, 256), 1)
    order = jnp.where(column == (row & 127) * 2 + (row >> 7), 1.0, 0.0).astype(jnp.bfloat16)
    loads[0].wait()
    mine = jnp.dot(order, base[...], preferred_element_type=jnp.float32).astype(jnp.bfloat16)
    for m in range(2):
        part = mine[m * 128 : (m + 1) * 128].reshape(STEPS, BLOCKS, 128)
        tab[0, :, 0, 0, :, m * 128 : (m + 1) * 128] = part
    order = jnp.where(column == (row & 63) * 4 + (row >> 6), 1.0, 0.0).astype(jnp.bfloat16)
    loads[1].wait()
    for half in range(2):
        mine = jnp.dot(
            order, grad[half * 256 : (half + 1) * 256], preferred_element_type=jnp.float32
        ).astype(jnp.bfloat16)
        for m in range(4):
            k = 1 + m // 2
            part = mine[m * 64 : (m + 1) * 64].reshape(4, BLOCKS, 128)
            tab[k, half * 4 : half * 4 + 4, 0, 0, :, m % 2 * 128 : m % 2 * 128 + 128] = part
    pl.semaphore_wait(barrier, len(partners))

    def remote(src, dst, send, recv, target):
        return pltpu.make_async_remote_copy(
            src_ref=src, dst_ref=dst, send_sem=send, recv_sem=recv, device_id=target, device_id_type=MESH
        )

    phase1, early, phase2, phase3, query, back = {}, {}, {}, {}, {}, {}
    for k, (d1, d2, d3) in enumerate(DIMS):
        for c, (s0, n) in enumerate(PIECES1):
            steps = pl.ds(s0, n)
            for by in NEAR:
                phase1[k, c, by] = remote(
                    tab.at[k, steps, 0, 0], tab.at[k, steps, 0, by],
                    send1.at[k, c, by - 1], recv1.at[k, c, by - 1], device(moved(d1, by), core),
                )
                early[k, c, by] = remote(
                    tab.at[k, steps, 0, 0], tab.at[k, steps, by, 0],
                    send1.at[k, c, by + 2], recv1.at[k, c, by + 2], device(moved(d2, by), core),
                )
        slot = here[d3] * 2 + core
        for c, (s0, n) in enumerate(PIECES2):
            for by in NEAR:
                phase2[k, c, by] = remote(
                    tab.at[k, pl.ds(s0, n), 0, pl.ds(1, 3)], tab.at[k, pl.ds(s0, n), by, pl.ds(1, 3)],
                    send2.at[k, c, by - 1], recv2.at[k, c, by - 1], device(moved(d2, by), core),
                )
        for c, (s0, n) in enumerate(PIECES):
            for i, (by, flip) in enumerate(LINE):
                place, which = moved(d3, by), (core + flip) % 2
                theirs = place[d3] * 2 + which
                phase3[k, c, i] = remote(
                    rep.at[k, theirs, pl.ds(s0, n)], rcv.at[k, slot, pl.ds(s0, n)],
                    send3.at[k, c, i], recv3.at[k, c, i], device(place, which),
                )
                if c == 0:
                    query[k, i] = remote(
                        ask.at[k, theirs // 4], asked.at[k, slot], sendq.at[k, i], recvq.at[k, i], device(place, which)
                    )
            back[k, c] = pltpu.make_async_copy(
                rep.at[k, slot, pl.ds(s0, n)], rcv.at[k, slot, pl.ds(s0, n)], back_sem.at[k, c]
            )

    for copies in (phase1, early):
        for c in range(len(PIECES1)):
            for by in NEAR:
                for k in range(3):
                    copies[k, c, by].start()

    loads[2].wait()
    loads[3].wait()
    lane = lax.broadcasted_iota(jnp.int32, (GROUPS, 128), 1)
    group = lax.broadcasted_iota(jnp.int32, (GROUPS, 128), 0)
    dev_columns = jnp.transpose(dev_ref[...].astype(jnp.float32))
    block_columns = jnp.transpose(block_ref[...].astype(jnp.float32))
    lane_f, group_f = lane.astype(jnp.float32), group.astype(jnp.float32)
    for s in range(STEPS):
        named = jnp.broadcast_to(dev_columns[:, s : s + 1], (GROUPS, 128)) == lane_f
        value = group_f * BLOCKS + jnp.broadcast_to(block_columns[:, s : s + 1], (GROUPS, 128))
        last = jnp.max(jnp.where(named, value, -1.0), axis=0, keepdims=True)
        least = jnp.min(jnp.where(named, value, 1e6), axis=0, keepdims=True)
        first[0, s : s + 1, :] = jnp.where(last >= 0.0, last - BLOCKS * jnp.floor(last * (1.0 / BLOCKS)), -1e4)
        first[1, s : s + 1, :] = jnp.where(least < last, least - BLOCKS * jnp.floor(least * (1.0 / BLOCKS)), -1e4)
    wide = lax.broadcasted_iota(jnp.int32, (8, 128), 1)
    for k, (d1, d2, d3) in enumerate(DIMS):
        for half in range(2):
            place = [None] * 3
            number = wide + half * 128
            place[d1], place[d2], place[d3] = (number >> 1) & 3, (number >> 3) & 3, (number >> 6) & 3
            index = owner_number(place, (number >> 5) & 1)
            chosen = jnp.where(
                (number & 1) == 0,
                jnp.take_along_axis(first[0], index, axis=1, mode="promise_in_bounds"),
                jnp.take_along_axis(first[1], index, axis=1, mode="promise_in_bounds"),
            )
            back_by = (((here[d2] - place[d2]) & 3) * 4 + ((here[d1] - place[d1]) & 3)) * BLOCKS
            ask[k, half] = chosen + back_by.astype(jnp.float32)
        for i in range(7):
            query[k, i].start()
        asked[k, here[d3] * 2 + core] = ask[k, here[d3] // 2]

    arrived = 0
    for c, (s0, n) in enumerate(PIECES2):
        while arrived < len(PIECES1) and PIECES1[arrived][0] < s0 + n:
            for k in range(3):
                for by in NEAR:
                    phase1[k, arrived, by].wait_recv()
            arrived += 1
        for by in NEAR:
            for k in range(3):
                phase2[k, c, by].start()

    dev_int = dev_columns.astype(jnp.int32)
    slot_lane = lax.broadcasted_iota(jnp.int32, (GROUPS, WIDTH), 1)
    for s in range(STEPS):
        same = (jnp.broadcast_to(dev_columns[:, s : s + 1], (GROUPS, 128)) == dev_ref[s : s + 1, :].astype(jnp.float32)) & (
            lane > group
        )
        rank = jnp.max(jnp.where(same, 1.0, 0.0), axis=1, keepdims=True).astype(jnp.int32)
        x, y, z, which = owner_parts(dev_int[:, s : s + 1])
        place = (x, y, z)
        for k, (d1, d2, d3) in enumerate(DIMS):
            slot = (((place[d3] * 2 + which) * 4 + place[d2]) * 4 + place[d1]) * 2 + rank
            sort[k, s] = jnp.where(jnp.broadcast_to(slot, (GROUPS, WIDTH)) == slot_lane, -1.0 / STEPS, 0.0).astype(jnp.bfloat16)

    loads[4].wait()

    @pl.loop(0, STEPS)
    def _(step):
        packed = pltpu.roll(cells[step, pl.ds(0, GROUPS, stride=GROUP_ROWS), :], 1, 1)
        for q in range(1, GROUP_ROWS):
            turned = pltpu.roll(cells[step, pl.ds(q, GROUPS, stride=GROUP_ROWS), :], 2 * q + 1, 1)
            packed = jnp.where(lane // 2 == q, turned, packed)
        edge_cells[step] = packed

    state[...] = jnp.zeros_like(state)
    edge[...] = jnp.zeros_like(edge)

    block_lane = lax.broadcasted_iota(jnp.int32, (WIDTH, WIDTH), 1).astype(jnp.float32)
    for k, (_, _, d3) in enumerate(DIMS):
        for i in range(7):
            query[k, i].wait_recv()
        window = (here[d3] * 2 + core) % 4
        halves = []
        for half in range(2):
            total = jnp.full((8, 128), -1e4, jnp.float32)
            for r in range(4):
                turned = pltpu.roll(asked[k, half * 4 + r], (r - window + 4) % 4 * 32, 1)
                total = jnp.where(wide // 32 == r, turned, total)
            halves.append(jnp.transpose(total))
        rows = jnp.concatenate(halves, axis=0)
        for s in range(STEPS):
            pick[k, s] = jnp.where(
                jnp.broadcast_to(rows[:, s : s + 1], (WIDTH, WIDTH)) == block_lane, 1.0, 0.0
            ).astype(jnp.bfloat16)

    arrived = sent = 0
    for c, (s0, n) in enumerate(PIECES2):
        while arrived < len(PIECES1) and PIECES1[arrived][0] < s0 + n:
            for k in range(3):
                for by in NEAR:
                    early[k, arrived, by].wait_recv()
            arrived += 1
        for k in range(3):
            for by in NEAR:
                phase2[k, c, by].wait_recv()
        while sent < len(PIECES) and sum(PIECES[sent]) <= s0 + n:
            for k in range(3):
                for s in range(PIECES[sent][0], sum(PIECES[sent])):
                    found = jnp.dot(pick[k, s], tab[k, s].reshape(WIDTH, WIDTH), preferred_element_type=jnp.float32)
                    rep[k, :, s] = found.astype(jnp.bfloat16).reshape(8, 32, WIDTH)
                for i in range(7):
                    phase3[k, sent, i].start()
                back[k, sent].start()
            sent += 1

    def collect(c):
        for k in range(3):
            back[k, c].wait()
            for i in range(7):
                phase3[k, c, i].wait_recv()

    def sort_blocks(step, at):
        for k in range(3):
            found = jnp.dot(sort[k, step], rcv[k, :, step].reshape(WIDTH, WIDTH), preferred_element_type=jnp.float32)
            coef[at, 2 * k] = found[:, :128]
            coef[at, 2 * k + 1] = found[:, 128:]

    def advance(at, start, index, px, py):
        vx, vy, gxx, gxy, gyx, gyy = (
            jnp.take_along_axis(coef[at, m, start : start + 8, :], index, axis=1, mode="promise_in_bounds")
            for m in range(6)
        )
        kx = vx + (gxx * px + gxy * py)
        ky = vy + (gyx * px + gyy * py)
        wx, wy = kx, ky
        for part in (0.25, 1.0 / 3.0, 0.5):
            wx, wy = kx + part * (gxx * wx + gxy * wy), ky + part * (gyx * wx + gyy * wy)
        return px + wx, py + wy

    def advance_edge(start, steps):
        rows = slice(start, start + 8)
        px, py = edge[0, rows, :], edge[1, rows, :]
        for at, step in steps:
            px, py = advance(at, start, edge_cells[step, rows, :], px, py)
        edge[0, rows, :], edge[1, rows, :] = px, py

    def advance_rows(start, steps):
        rows = slice(start, start + 8)
        for q in range(GROUP_ROWS):
            px, py = state[0, q, rows, :], state[1, q, rows, :]
            for at, step in steps:
                index = cells[step, pl.ds(start * GROUP_ROWS + q, 8, stride=GROUP_ROWS), :]
                px, py = advance(at, start, index, px, py)
            state[0, q, rows, :], state[1, q, rows, :] = px, py

    for c, (s0, n) in enumerate(PIECES[:-1]):
        collect(c)

        @pl.loop(s0, s0 + n)
        def _(step):
            sort_blocks(step, 0)
            for start in range(0, GROUPS, 8):
                advance_edge(start, [(0, step)])
                advance_rows(start, [(0, step)])

    s0, n = PIECES[-1]
    collect(len(PIECES) - 1)
    steps = [(i, s0 + i) for i in range(n)]
    for at, step in steps:
        sort_blocks(step, at)
    for start in range(0, GROUPS, 8):
        advance_edge(start, steps)
    for comp in range(2):
        cols_out[comp] = jnp.transpose(edge[comp])[:8, :]
    halo = []
    for i, lon_to in enumerate((east, west)):
        halo.append(remote(cols_out, cols_in.at[i], sendh.at[i], recvh.at[i], (lon_to, lat)))
        halo[-1].start()
    for start in (0, GROUPS - 8):
        advance_rows(start, steps)
    rows_out[...] = jnp.zeros_like(rows_out)
    for comp in range(2):
        rows_out[comp : comp + 1, :] = state[comp, 0, 0:1, :]
        rows_out[2 + comp : 3 + comp, :] = state[comp, GROUP_ROWS - 1, GROUPS - 1 : GROUPS, :]
    for i, by in enumerate((1, 3)):
        halo.append(remote(rows_out, rows_in.at[i], sendh.at[2 + i], recvh.at[2 + i], device(moved(2, by), core)))
        halo[-1].start()
    for start in range(8, GROUPS - 8, 8):
        advance_rows(start, steps)
    for comp in range(2):
        for q in range(GROUP_ROWS):
            flow[comp, pl.ds(q, GROUPS, stride=GROUP_ROWS), :] = state[comp, q]
    for copies in (phase1, early, phase2, phase3, query):
        for copy in copies.values():
            copy.wait_send()
    for copy in halo:
        copy.wait_send()
        copy.wait_recv()


def stretch_kernel(state, rows_in, cols_in, rows_out, flow, flow_hbm, ftle_hbm, ftle, sem):
    lat = lax.axis_index("lat")
    flow_copy = pltpu.make_async_copy(flow, flow_hbm, sem.at[0])
    flow_copy.start()
    lane = lax.broadcasted_iota(jnp.int32, (GROUPS, 128), 1)
    group = lax.broadcasted_iota(jnp.int32, (GROUPS, 128), 0)
    south_own, north_own = lat == 0, lat == 3
    at_west, at_east = lane == 0, lane == 127
    bottom, top = group == 0, group == GROUPS - 1
    diffs = {}
    for comp in range(2):
        south = jnp.where(south_own, rows_out[comp : comp + 1, :], rows_in[0, 2 + comp : 3 + comp, :])
        north = jnp.where(north_own, rows_out[2 + comp : 3 + comp, :], rows_in[1, comp : comp + 1, :])
        from_west, from_east = jnp.transpose(cols_in[0, comp]), jnp.transpose(cols_in[1, comp])
        for q in range(GROUP_ROWS):
            own_rows = state[comp, q]
            west_column = from_west[:, 2 * q : 2 * q + 1]
            east_column = from_east[:, 2 * q + 1 : 2 * q + 2]
            low = jnp.where(at_west, west_column, pltpu.roll(own_rows, 1, 1))
            high = jnp.where(at_east, east_column, pltpu.roll(own_rows, 127, 1))
            diffs[comp, q, 0] = (high - low) * 0.5
            if q == 0:
                below = jnp.where(bottom, south, pltpu.roll(state[comp, GROUP_ROWS - 1], 1, 0))
            else:
                below = state[comp, q - 1]
            if q == GROUP_ROWS - 1:
                above = jnp.where(top, north, pltpu.roll(state[comp, 0], GROUPS - 1, 0))
            else:
                above = state[comp, q + 1]
            diffs[comp, q, 1] = (above - below) * 0.5
    for q in range(GROUP_ROWS):
        map_xx, map_yx = 1.0 + diffs[0, q, 0], diffs[1, q, 0]
        map_xy, map_yy = diffs[0, q, 1], 1.0 + diffs[1, q, 1]
        green_xx = map_xx * map_xx + map_yx * map_yx
        green_yy = map_xy * map_xy + map_yy * map_yy
        green_xy = map_xx * map_xy + map_yx * map_yy
        half_diff = 0.5 * (green_xx - green_yy)
        largest = 0.5 * (green_xx + green_yy) + jnp.sqrt(half_diff * half_diff + green_xy * green_xy)
        ftle[pl.ds(q, GROUPS, stride=GROUP_ROWS), :] = 0.5 * jnp.log(largest)
    ftle_copy = pltpu.make_async_copy(ftle, ftle_hbm, sem.at[1])
    ftle_copy.start()
    flow_copy.wait()
    ftle_copy.wait()


def body(vel_base, vel_grad, route_dev, route_block, seed_cells):
    dma = pltpu.SemaphoreType.DMA
    vmem = pl.BlockSpec(memory_space=pltpu.VMEM)
    hbm = pl.BlockSpec(memory_space=pltpu.HBM)
    bf16, f32, i32 = jnp.bfloat16, jnp.float32, jnp.int32
    moved = pl.pallas_call(
        advect_kernel,
        out_shape=(
            jax.ShapeDtypeStruct((2, GROUP_ROWS, GROUPS, 128), f32),
            jax.ShapeDtypeStruct((2, 8, 128), f32),
            jax.ShapeDtypeStruct((2, 2, 8, 128), f32),
            jax.ShapeDtypeStruct((8, 128), f32),
            jax.ShapeDtypeStruct((2, 512, 128), f32),
        ),
        in_specs=[hbm] * 5,
        out_specs=(vmem,) * 5,
        scratch_shapes=[
            pltpu.VMEM((256, 128), bf16),
            pltpu.VMEM((512, 128), bf16),
            pltpu.VMEM((STEPS, GROUPS), i32),
            pltpu.VMEM((STEPS, GROUPS), i32),
            pltpu.VMEM((STEPS, 512, 128), i32),
            pltpu.VMEM((3, STEPS, 4, 4, BLOCKS, WIDTH), bf16),
            pltpu.VMEM((3, STEPS, 8, 32, WIDTH), bf16),
            pltpu.VMEM((3, STEPS, 8, 32, WIDTH), bf16),
            pltpu.VMEM((3, STEPS, WIDTH, WIDTH), bf16),
            pltpu.VMEM((3, STEPS, GROUPS, WIDTH), bf16),
            pltpu.VMEM((3, 2, 8, 128), f32),
            pltpu.VMEM((3, 8, 8, 128), f32),
            pltpu.VMEM((2, STEPS, 128), f32),
            pltpu.VMEM((PIECES[-1][1], 6, GROUPS, 128), f32),
            pltpu.VMEM((STEPS, GROUPS, 128), i32),
            pltpu.VMEM((2, GROUPS, 128), f32),
            pltpu.VMEM((2, 8, 128), f32),
            dma((5,)), dma((3, len(PIECES))),
            dma((3, len(PIECES1), 6)), dma((3, len(PIECES1), 6)),
            dma((3, len(PIECES2), 3)), dma((3, len(PIECES2), 3)),
            dma((3, len(PIECES), 7)), dma((3, len(PIECES), 7)),
            dma((3, 7)), dma((3, 7)),
            dma((4,)), dma((4,)),
        ],
        compiler_params=pltpu.CompilerParams(collective_id=0, has_side_effects=True, vmem_limit_bytes=48 << 20),
    )(
        *(pltpu.with_memory_space_constraint(a, pltpu.HBM) for a in (
        vel_base.reshape(256, 128), vel_grad.reshape(512, 128), route_dev.reshape(STEPS, GROUPS),
        route_block.reshape(STEPS, GROUPS), seed_cells)),
    )
    return pl.pallas_call(
        stretch_kernel,
        out_shape=(jax.ShapeDtypeStruct((2, 512, 128), f32), jax.ShapeDtypeStruct((512, 128), f32)),
        in_specs=[vmem] * 5,
        out_specs=(hbm, hbm),
        scratch_shapes=[pltpu.VMEM((512, 128), f32), dma((2,))],
        compiler_params=pltpu.CompilerParams(vmem_limit_bytes=6 << 20),
    )(*moved)


def solution(mesh):
    in_specs = (
        P("lon", "lat", None, None, None, None),
        P("lon", "lat", None, None, None, None),
        P("lon", "lat", None, None, None),
        P("lon", "lat", None, None),
        P(None, "lat", "lon"),
    )
    out_specs = (P(None, "lat", "lon"), P("lat", "lon"))
    return jax.shard_map(body, mesh=mesh, in_specs=in_specs, out_specs=out_specs, check_vma=False)
```
